32 devices in a mesh: col: 4 (over y, x), tile: 8 (over z, core).
Axes of the slice: x: 2, y: 2, z: 4, core: 2. Of those that a mesh axis runs over, the one named last changes fastest.
Arguments:
- vectors: float32 [8, 4, 64, 2048], P(None, None, 'tile', 'col'), may hold values from -12 to 12
- onsite: float32 [4, 64, 2048], P(None, 'tile', 'col'), may hold values from -0.3 to 0.3
- intra_hop: float32 [3, 2, 64, 2048], P(None, None, 'tile', 'col'), may hold values from 0.15 to 0.35
- inter_index: int32 [4, 2, 64, 2048], P(None, None, 'tile', 'col'), may hold values from 0 to 18
- inter_hop: float32 [4, 2, 64, 2048], P(None, None, 'tile', 'col'), may hold values from 0.04 to 0.16
Outputs:
- last_term: float32 [8, 4, 64, 2048], P(None, None, 'tile', 'col')
- moments: float32 [7, 8], replicated
The draws below stay inside these ranges and needn't reach their ends.
Inputs may be any that keep to these rules, and one draw needn't show every extreme that they name: `inter_index`: A code c below 18 names the second-layer orbital of sublattice c // 9 in the cell at offset ((c % 9) // 3 - 1, c % 3 - 1) from the slot's cell; 18 marks an empty slot.
All inputs are finite; a program needn't handle non-finite values.
Results may differ from the reference program's by a relative error of at most 0.000025.
Values sent between devices are 32-bit elements; how exact they have to be, the bound alone decides.
A program may use at most 64 MiB of HBM per device.

```python
import jax
import jax.numpy as jnp

VECS = 8
K = 4
NA = 64
NB = 2048


def draw_vectors(key, part):
    first_key = jax.random.fold_in(jax.random.fold_in(key, 7), 0)
    positions = jnp.arange(NA, dtype=jnp.float32) / NA
    ramp = jnp.exp(jnp.log(3.0) * positions)[:, None]
    base = jnp.clip(jax.random.normal(first_key, (VECS, 4, NA, NB), jnp.float32), -4.0, 4.0)
    return base * ramp


def touch_ends(values, key, low, largest):
    index_at = [jax.random.randint(jax.random.fold_in(key, axis), (), 0, length) for axis, length in enumerate(values.shape)]
    longest = values.shape.index(max(values.shape))
    neighbour = index_at[:longest] + [(index_at[longest] + 1) % values.shape[longest]] + index_at[longest + 1:]
    return values.at[tuple(index_at)].set(low).at[tuple(neighbour)].set(largest)


def shard_levels(own_key, extent, cuts, least, high):
    def one(axis_at, shards_of):
        draws = jax.random.uniform(jax.random.fold_in(jax.random.fold_in(own_key, 6), axis_at), (shards_of,), jnp.float32, least / len(cuts), high / len(cuts))
        return jnp.repeat(jnp.exp(draws), extent[axis_at] // shards_of).reshape((-1,) + (1,) * (len(extent) - axis_at - 1))

    level = one(*cuts[0])
    for cut in cuts[1:]:
        level = level * one(*cut)
    return level


def setup_inputs(seed: int = 0) -> dict:
    seeds = jax.random.split(jax.random.key(seed), 6)
    vectors = draw_vectors(jax.random.fold_in(seeds[5], 71), 0)
    onsite = jnp.clip(jax.random.uniform(seeds[1], (4, NA, NB), jnp.float32, -0.3, 0.3) * shard_levels(seeds[1], (4, NA, NB), ((1, 8), (2, 4)), -0.4, 0.0), -0.3, 0.3)
    intra_hop = jnp.clip(0.15 + 0.19999999 * jax.random.uniform(seeds[2], (3, 2, NA, NB), jnp.float32) ** shard_levels(seeds[2], (3, 2, NA, NB), ((2, 8), (3, 4)), -0.2, 0.2), 0.15, 0.35)
    inter_index = touch_ends(jax.random.randint(seeds[3], (K, 2, NA, NB), 0, 19), jax.random.fold_in(seeds[3], 1), 0, 18).astype(jnp.int32)
    inter_hop = jnp.clip(0.04 + 0.12 * jax.random.uniform(seeds[4], (K, 2, NA, NB), jnp.float32) ** shard_levels(seeds[4], (K, 2, NA, NB), ((2, 8), (3, 4)), -0.2, 0.2), 0.04, 0.16)
    return {"vectors": vectors, "onsite": onsite, "intra_hop": intra_hop, "inter_index": inter_index, "inter_hop": inter_hop}


BOND_OFFSETS = ((0, 0), (-1, 0), (0, -1))


def rolled(array, row_off, col_off):
    return jnp.roll(array, (-row_off, -col_off), axis=(-2, -1))


def make_weights(neighbours, amplitude):
    return jnp.stack([jnp.sum(jnp.where(neighbours == code_no, amplitude, jnp.zeros_like(amplitude)), axis=0) for code_no in range(18)], axis=1)


def apply_hamiltonian(vector, onsite, intra_hop, weights, pick):
    outputs = []
    for layer_no in range(2):
        side_a = vector[:, 2 * layer_no]
        side_b = vector[:, 2 * layer_no + 1]
        out_a = pick(onsite[2 * layer_no], 0, 0) * pick(side_a, 0, 0)
        out_b = pick(onsite[2 * layer_no + 1], 0, 0) * pick(side_b, 0, 0)
        for bond_idx in range(3):
            row_off, col_off = BOND_OFFSETS[bond_idx]
            out_a = out_a + pick(intra_hop[bond_idx, layer_no], 0, 0) * pick(side_b, row_off, col_off)
            out_b = out_b + pick(intra_hop[bond_idx, layer_no], -row_off, -col_off) * pick(side_a, -row_off, -col_off)
        outputs += [out_a, out_b]
    for source in range(2):
        for code_no in range(18):
            target = code_no // 9
            row_off = (code_no % 9) // 3 - 1
            col_off = code_no % 3 - 1
            outputs[source] = outputs[source] + pick(weights[source, code_no], 0, 0) * pick(vector[:, 2 + target], row_off, col_off)
            outputs[2 + target] = outputs[2 + target] + pick(weights[source, code_no], -row_off, -col_off) * pick(vector[:, source], -row_off, -col_off)
    return jnp.stack(outputs, axis=1)


def inner_sums(left, right):
    return jnp.sum(left * right, axis=(1, 2, 3))


def moments_from(totals, orbitals):
    scaled = totals / orbitals
    zeroth = scaled[0]
    first = scaled[1]
    return jnp.stack([zeroth, first, 2.0 * scaled[2] - zeroth, 2.0 * scaled[3] - first, 2.0 * scaled[4] - zeroth, 2.0 * scaled[5] - first, 2.0 * scaled[6] - zeroth])


def reference(vectors, onsite, intra_hop, inter_index, inter_hop):
    weights = make_weights(inter_index, inter_hop)

    def operator(vector):
        return apply_hamiltonian(vector, onsite, intra_hop, weights, rolled)

    term_zero = vectors
    term_one = operator(term_zero)
    term_two = 2.0 * operator(term_one) - term_zero
    last_term = 2.0 * operator(term_two) - term_one
    totals = jnp.stack([inner_sums(term_zero, term_zero), inner_sums(term_one, term_zero), inner_sums(term_one, term_one), inner_sums(term_two, term_one), inner_sums(term_two, term_two), inner_sums(last_term, term_two), inner_sums(last_term, last_term)])
    return last_term, moments_from(totals, 4 * NA * NB)
```

```python
import functools

import jax
import jax.numpy as jnp
from jax import lax
from jax.experimental import pallas as pl
from jax.experimental.pallas import tpu as pltpu
from jax.sharding import PartitionSpec as P

RIM = 2
LANES = 128
CODES = 18
MESH = pl.DeviceIdType.MESH
BONDS = ((0, 0), (-1, 0), (0, -1))
HOP, CODE, SITE, BOND2 = 4, 5, 6, 7


def kernel(
    n_col, n_tile, orbitals,
    v_hbm, onsite_hbm, intra_hbm, index_hbm, hop_hbm,
    out_ref, mom_ref,
    v_ref, onsite_ref, intra_ref, index_ref, hop_ref, load_sem,
    area, term1, term2, term3, moved0, moved1, moved2, weights, weights_t, bond_t,
    packs, halo, sums, part, all_parts,
    row_send, row_recv, pack_send, pack_recv, part_send, part_recv,
):
    rows = v_ref.shape[2]
    cols = v_ref.shape[3]
    blocks = cols // LANES
    ring = cols + LANES
    my_col = lax.axis_index("col")
    my_tile = lax.axis_index("tile")
    lane = lax.broadcasted_iota(jnp.int32, (8, LANES), 1)
    sub = lax.broadcasted_iota(jnp.int32, (8, LANES), 0)

    def col_at(step):
        return lax.rem(my_col + step + n_col, n_col)

    def tile_at(step):
        return lax.rem(my_tile + step + n_tile, n_tile)

    loads = [
        pltpu.make_async_copy(src, dst, load_sem.at[n])
        for n, (src, dst) in enumerate(
            (
                (v_hbm, v_ref),
                (hop_hbm, hop_ref),
                (index_hbm, index_ref),
                (onsite_hbm, onsite_ref),
                (intra_hbm, intra_ref),
            )
        )
    ]
    for load in loads:
        load.start()

    barrier = pltpu.get_barrier_semaphore()
    devices = n_col * n_tile
    me = my_col * n_tile + my_tile

    def device(step):
        at = lax.rem(me + step, devices)
        return (lax.div(at, n_tile), lax.rem(at, n_tile))

    def greet(i, carry):
        pl.semaphore_signal(barrier, inc=1, device_id=device(i), device_id_type=MESH)
        return carry

    lax.fori_loop(1, devices, greet, 0)

    for load in loads:
        load.wait()
    own = slice(RIM, RIM + rows)
    for o in range(4):
        area[o, own, :, 0:cols] = jnp.swapaxes(v_ref[:, o], 0, 1)
    area[HOP, own, :, 0:cols] = jnp.swapaxes(hop_ref[...], 0, 1)
    area[CODE, own, :, 0:cols] = jnp.swapaxes(index_ref[...].astype(jnp.float32), 0, 1)
    area[SITE, own, :, 0:cols] = jnp.swapaxes(
        jnp.concatenate([onsite_ref[...], intra_ref[0:4]], axis=0), 0, 1
    )
    area[BOND2, own, :, 0:cols] = jnp.swapaxes(
        jnp.concatenate([intra_ref[4:6], jnp.zeros((6, rows, cols), jnp.float32)], axis=0), 0, 1
    )

    first, last, half = lane == 0, lane == LANES - 1, lane < LANES // 2
    slot_of = lane // 4
    terms = (term1, term2, term3)
    moved = (moved0, moved1, moved2)

    def block(b):
        return slice(b * LANES, (b + 1) * LANES)

    def pack(r, carry):
        out = list(carry)
        for g in range(8):
            i = (g % 4) * rows + r
            edges = jnp.where(half, area[g, RIM + r, :, 0:LANES], area[g, RIM + r, :, cols - LANES : cols])
            edges = pltpu.roll(edges, 4 * i, 1)
            out[g // 4] = jnp.where(slot_of == i, edges, out[g // 4])
            out[2 + g // 4] = jnp.where(
                slot_of == lax.rem(i + LANES // 4 - 1, LANES // 4), edges, out[2 + g // 4]
            )
        return tuple(out)

    zero = jnp.zeros((8, LANES), jnp.float32)
    packed = lax.fori_loop(0, rows, pack, (zero,) * 4)
    for n in range(4):
        packs[n // 2, n % 2] = packed[n]

    code_of = [(3 * sub + g).astype(jnp.float32) for g in range(3)]

    def weigh(r, s, b):
        at = block(b)
        total = [None] * 3
        for k in range(4):
            f = 2 * k + s
            code = jnp.broadcast_to(area[CODE, r, f : f + 1, at], (8, LANES))
            hop = jnp.broadcast_to(area[HOP, r, f : f + 1, at], (8, LANES))
            for g in range(3):
                x = jnp.where(code == code_of[g], hop, 0.0)
                total[g] = x if k == 0 else total[g] + x
        for g in range(3):
            weights[r, s, 8 * g : 8 * g + 8, at] = total[g]
        return total

    def back(x):
        return pltpu.roll(x, 1, 1)

    def ahead(x):
        return pltpu.roll(x, LANES - 1, 1)

    def loop(low, high, body):
        def step(i, carry):
            body(i)
            return carry

        lax.fori_loop(low, high, step, 0)

    low, high = RIM, RIM + rows
    def put(ref, at, b, x):
        ref[(*at, slice(None), block(b))] = x

    def own_turns(xs, way, store):
        if way < 0:
            ys = [back(x) for x in xs]
            for b in range(blocks):
                store(b, ys[b] if b == 0 else jnp.where(first, ys[b - 1], ys[b]))
        else:
            ys = [ahead(x) for x in xs]
            for b in range(blocks):
                store(b, ys[b] if b == blocks - 1 else jnp.where(last, ys[b + 1], ys[b]))

    def ring_turns(xs, way, store, count):
        if way < 0:
            ys = [back(x) for x in xs]
            for b in range(count):
                store(b, jnp.where(first, ys[b - 1], ys[b]))
        else:
            ys = [ahead(x) for x in xs]
            for b in range(count):
                store(b, jnp.where(last, ys[(b + 1) % (blocks + 1)], ys[b]))

    def edge_turns(x0, x3, x4, way, load, store):
        if way < 0:
            y3, y4 = back(x3), back(x4)
            store(0, jnp.where(first, y4, load(0)))
            store(blocks, jnp.where(first, y3, y4))
        else:
            y0, y4 = ahead(x0), ahead(x4)
            store(blocks - 1, jnp.where(last, y4, load(blocks - 1)))
            store(blocks, jnp.where(last, y0, y4))

    def field(g, r):
        return [area[g, r, :, block(b)] for b in range(blocks + 1)]

    def moved_at(ref, at):
        return lambda b, x: put(ref, at, b, x)

    def weights_at(r, s, g):
        def store(b, x):
            weights_t[r, s, 8 * g : 8 * g + 8, block(b)] = x
        return store

    def bond_at(r):
        def store(b, x):
            bond_t[r, :, block(b)] = x
        return store

    def prepare_own(r):
        for s in range(2):
            totals = [weigh(r, s, b) for b in range(blocks)]
            own_turns([t[0] for t in totals], 1, weights_at(r, s, 0))
            own_turns([t[2] for t in totals], -1, weights_at(r, s, 1))
        for o in range(4):
            xs = field(o, r)[:blocks]
            own_turns(xs, -1, moved_at(moved0, (0, o, r)))
            own_turns(xs, 1, moved_at(moved0, (1, o, r)))
        own_turns(field(BOND2, r)[:blocks], 1, bond_at(r))

    def unpack(r, theirs, dt, groups):
        for g in range(groups):
            i = (g % 4) * rows + theirs
            both = jnp.where(slot_of == i, halo[1 + dt, g // 4], halo[4 + dt, g // 4])
            area[g, r, :, cols:ring] = pltpu.roll(both, lax.rem(LANES - 4 * i, LANES), 1)

    def prepare_edges(r):
        unpack(r, r - low, 0, 8)
        b0, b3, b4 = block(0), block(blocks - 1), block(blocks)
        for s in range(2):
            total = weigh(r, s, blocks)
            for g, way in ((0, 1), (2, -1)):
                rows_of = slice(8 * g, 8 * g + 8)
                half_of = slice(4 * g, 4 * g + 8)
                edge_turns(
                    weights[r, s, rows_of, b0], weights[r, s, rows_of, b3], total[g], way,
                    lambda b, half_of=half_of, s=s: weights_t[r, s, half_of, block(b)],
                    weights_at(r, s, g // 2),
                )
        for o in range(4):
            x0, x3, x4 = area[o, r, :, b0], area[o, r, :, b3], area[o, r, :, b4]
            for side, way in ((0, -1), (1, 1)):
                edge_turns(
                    x0, x3, x4, way,
                    lambda b, o=o, side=side: moved0[side, o, r, :, block(b)],
                    moved_at(moved0, (side, o, r)),
                )
        edge_turns(
            area[BOND2, r, :, b0], None, area[BOND2, r, :, b4], 1,
            lambda b: bond_t[r, :, block(b)], bond_at(r),
        )

    def prepare(r, theirs, dt, groups):
        unpack(r, theirs, dt, groups)
        for s in range(2):
            totals = [weigh(r, s, b) for b in range(blocks + 1)]
            ring_turns([t[0] for t in totals], 1, weights_at(r, s, 0), blocks + 1)
            ring_turns([t[2] for t in totals], -1, weights_at(r, s, 1), blocks + 1)
        for o in range(4):
            xs = field(o, r)
            ring_turns(xs, -1, moved_at(moved0, (0, o, r)), blocks + 1)
            ring_turns(xs, 1, moved_at(moved0, (1, o, r)), blocks + 1)
        if groups == 8:
            ring_turns(field(BOND2, r), 1, bond_at(r), blocks + 1)

    for n in range(7):
        sums[n] = zero

    pl.semaphore_wait(barrier, devices - 1)

    pack_copies = []
    for side, step in ((0, -1), (1, 1)):
        for dt in (0, -1, 1):
            slot = side * 3 + 1 - dt
            copy = pltpu.make_async_remote_copy(
                src_ref=packs.at[side],
                dst_ref=halo.at[slot],
                send_sem=pack_send.at[slot],
                recv_sem=pack_recv.at[slot],
                device_id=(col_at(step), tile_at(dt)),
                device_id_type=MESH,
            )
            copy.start()
            pack_copies.append(copy)

    rim_copies = []

    def send_rim(layer, way, src, dst):
        copy = pltpu.make_async_remote_copy(
            src_ref=src,
            dst_ref=dst,
            send_sem=row_send.at[layer, way],
            recv_sem=row_recv.at[layer, way],
            device_id=(my_col, tile_at(1 - 2 * way)),
            device_id_type=MESH,
        )
        copy.start()
        rim_copies.append(copy)

    for layer in range(2):
        for way in range(2):
            src, dst = ((high - 1 - layer, low - 1 - layer), (low + layer, high + layer))[way]
            groups = 8 if layer == 0 else 6 + way
            send_rim(
                layer, way,
                area.at[0:groups, src : src + 1, :, 0:cols],
                area.at[0:groups, dst : dst + 1, :, 0:cols],
            )

    loop(low, high, prepare_own)

    def term(k, o, r, at):
        return area[o, r, :, at] if k == 0 else terms[k - 1][o, r, :, at]

    def hamiltonian(k, r, at):
        def v(o, row_off, col_off):
            if col_off == 0:
                return term(k, o, r + row_off, at)
            return moved[k][(col_off + 1) // 2, o, r + row_off, :, at]

        def spread(x):
            return jnp.broadcast_to(x, (8, LANES))

        def site(f, row):
            return spread(area[SITE, row, f : f + 1, at])

        outs = []
        for l in range(2):
            a, b = 2 * l, 2 * l + 1
            f0, f1 = site(4 + l, r), site(6 + l, r)
            f2 = spread(area[BOND2, r, l : l + 1, at])
            outs.append(
                site(a, r) * v(a, 0, 0) + f0 * v(b, 0, 0) + f1 * v(b, -1, 0) + f2 * v(b, 0, -1)
            )
            outs.append(
                site(b, r) * v(b, 0, 0)
                + f0 * v(a, 0, 0)
                + site(6 + l, r + 1) * v(a, 1, 0)
                + spread(bond_t[r, l : l + 1, at]) * v(a, 0, 1)
            )
        for s in range(2):
            for c in range(CODES):
                t, e, f = c // 9, c % 9 // 3 - 1, c % 3 - 1
                n = 8 * (f + 1) + 3 * t + e + 1
                outs[s] = outs[s] + spread(weights[r, s, n : n + 1, at]) * v(2 + t, e, f)
                if f == 0:
                    other = weights[r - e, s, n : n + 1, at]
                else:
                    n = 4 * (f + 1) + 3 * t + e + 1
                    other = weights_t[r - e, s, n : n + 1, at]
                outs[2 + t] = outs[2 + t] + spread(other) * v(s, -e, -f)
        return outs

    def advance(k, r):
        inside = jnp.where((r >= RIM) & (r < RIM + rows), 1.0, 0.0).astype(jnp.float32)
        cross, square, first_sum = zero, zero, zero
        turns = [{} for _ in range(4)]

        def store_turn(o, way, b):
            near, far = turns[o][b], turns[o][(b + way) % (blocks + 1)]
            if way < 0:
                x = jnp.where(first, far[0], near[0])
            else:
                x = jnp.where(last, far[1], near[1])
            moved[k + 1][(way + 1) // 2, o, r, :, block(b)] = x

        for b in ([blocks] if k < 2 else []) + list(range(blocks)):
            at = block(b)
            outs = hamiltonian(k, r, at)
            for o in range(4):
                old = term(k, o, r, at)
                new = outs[o] if k == 0 else 2.0 * outs[o] - term(k - 1, o, r, at)
                terms[k][o, r, :, at] = new
                if b < blocks:
                    cross = cross + new * old
                    square = square + new * new
                    if k == 0:
                        first_sum = first_sum + old * old
                if k < 2:
                    turns[o][b] = (back(new), ahead(new))
                    if b < blocks:
                        store_turn(o, -1, b)
                    if 0 < b < blocks:
                        store_turn(o, 1, b - 1)
                    if b == 0 and k == 0:
                        store_turn(o, 1, blocks)
        if k < 2:
            for o in range(4):
                store_turn(o, 1, blocks - 1)
                if k == 0:
                    store_turn(o, -1, blocks)
        if k == 0:
            sums[0] += inside * first_sum
        sums[2 * k + 1] += inside * cross
        sums[2 * k + 2] += inside * square

    for n in (0, 3):
        pack_copies[n].wait_recv()
    loop(low, high, prepare_edges)
    for k in range(3):
        loop(low + 1 + k, high - 1 - k, functools.partial(advance, k))
        if k == 1:
            send_rim(2, 0, term1.at[:, high - 2 : high - 1], term1.at[:, 0:1])
            send_rim(2, 1, term1.at[:, low + 1 : low + 2], term1.at[:, high + 1 : high + 2])

    for n in (1, 2, 4, 5):
        pack_copies[n].wait_recv()
    for layer in range(3):
        for way in range(2):
            rim_copies[2 * layer + way].wait_recv()
        if layer < 2:
            prepare(low - 1 - layer, rows - 1 - layer, -1, 8 if layer == 0 else 6)
            prepare(high + layer, layer, 1, 8 if layer == 0 else 7)
        else:
            for r in (0, high + 1):
                for o in range(4):
                    xs = [term1[o, r, :, block(b)] for b in range(blocks + 1)]
                    ring_turns(xs, -1, moved_at(moved1, (0, o, r)), blocks + 1)
                    ring_turns(xs, 1, moved_at(moved1, (1, o, r)), blocks + 1)
        for k in range(1 if layer == 2 else 0, 3):
            top, bottom = low - layer + k, high - 1 + layer - k
            loop(0, 2, lambda i, k=k: advance(k, top + i * (bottom - top)))

    row = jnp.zeros((8, LANES), jnp.float32)
    for n in range(7):
        total = jnp.sum(sums[n], axis=1, keepdims=True)
        row = jnp.where(lane == sub + 8 * n, jnp.broadcast_to(total, (8, LANES)), row)
    part[...] = jnp.sum(row, axis=0, keepdims=True)
    all_parts[me] = part[...]

    def part_copy(step):
        return pltpu.make_async_remote_copy(
            src_ref=part,
            dst_ref=all_parts.at[me],
            send_sem=part_send,
            recv_sem=part_recv,
            device_id=device(step),
            device_id_type=MESH,
        )

    loop(1, devices, lambda i: part_copy(i).start())
    for o in range(4):
        out_ref[:, o] = jnp.swapaxes(term3[o, own, :, 0:cols], 0, 1)

    for copy in rim_copies + pack_copies:
        copy.wait_send()
    arrived = pltpu.make_async_remote_copy(
        src_ref=all_parts.at[1:devices],
        dst_ref=all_parts.at[1:devices],
        send_sem=part_send,
        recv_sem=part_recv,
        device_id=device(1),
        device_id_type=MESH,
    )
    arrived.wait_recv()
    arrived.wait_send()
    pieces = [all_parts[n] for n in range(devices)]
    while len(pieces) > 1:
        half_way = (len(pieces) + 1) // 2
        pieces = [
            pieces[n] + pieces[n + half_way] if n + half_way < len(pieces) else pieces[n]
            for n in range(half_way)
        ]
    total = pieces[0]
    total = jnp.broadcast_to(total / orbitals, (8, LANES))
    scaled = [pltpu.roll(total, (LANES - 8 * n) % LANES, 1)[0:1, 0:8] for n in range(7)]
    mom_ref[0:1, :] = scaled[0]
    mom_ref[1:2, :] = scaled[1]
    for n in range(2, 7):
        mom_ref[n : n + 1, :] = 2.0 * scaled[n] - scaled[n % 2]


def emit(last_ref, rows_ref, out_ref, mom_ref, sem):
    copies = [
        pltpu.make_async_copy(last_ref, out_ref, sem.at[0]),
        pltpu.make_async_copy(rows_ref, mom_ref, sem.at[1]),
    ]
    for copy in copies:
        copy.start()
    for copy in copies:
        copy.wait()


def on_device(n_col, n_tile, vectors, onsite, intra_hop, inter_index, inter_hop):
    count, _, rows, cols = vectors.shape
    slots = inter_index.shape[0]
    assert count == 8 and slots == 4 and rows == 8 and cols % LANES == 0
    tall = rows + 2 * RIM
    ring = cols + LANES
    f32 = jnp.float32
    vmem = pl.BlockSpec(memory_space=pltpu.VMEM)
    dma = pltpu.SemaphoreType.DMA
    results = pl.pallas_call(
        functools.partial(kernel, n_col, n_tile, 4 * rows * cols * n_col * n_tile),
        out_shape=(
            jax.ShapeDtypeStruct(vectors.shape, f32),
            jax.ShapeDtypeStruct((7, count), f32),
        ),
        in_specs=[pl.BlockSpec(memory_space=pltpu.HBM)] * 5,
        out_specs=(vmem, vmem),
        scratch_shapes=[
            pltpu.VMEM(vectors.shape, f32),
            pltpu.VMEM(onsite.shape, f32),
            pltpu.VMEM((6, rows, cols), f32),
            pltpu.VMEM((2 * slots, rows, cols), jnp.int32),
            pltpu.VMEM((2 * slots, rows, cols), f32),
            dma((5,)),
            pltpu.VMEM((8, tall, 8, ring), f32),
            *[pltpu.VMEM((4, tall, 8, ring), f32)] * 3,
            *[pltpu.VMEM((2, 4, tall, 8, ring), f32)] * 3,
            pltpu.VMEM((tall, 2, 24, ring), f32),
            pltpu.VMEM((tall, 2, 16, ring), f32),
            pltpu.VMEM((tall, 8, ring), f32),
            pltpu.VMEM((2, 2, 8, LANES), f32),
            pltpu.VMEM((6, 2, 8, LANES), f32),
            pltpu.VMEM((7, 8, LANES), f32),
            pltpu.VMEM((1, LANES), f32),
            pltpu.VMEM((n_col * n_tile, 1, LANES), f32),
            dma((3, 2)), dma((3, 2)), dma((6,)), dma((6,)), dma, dma,
        ],
        compiler_params=pltpu.CompilerParams(
            collective_id=0, has_side_effects=True, vmem_limit_bytes=32 << 20
        ),
    )(
        *(
            pltpu.with_memory_space_constraint(x, pltpu.HBM)
            for x in (
                vectors,
                onsite,
                intra_hop.reshape(6, rows, cols),
                inter_index.reshape(2 * slots, rows, cols),
                inter_hop.reshape(2 * slots, rows, cols),
            )
        )
    )
    kept = pl.BlockSpec(memory_space=pl.ANY)
    return pl.pallas_call(
        emit,
        out_shape=(
            jax.ShapeDtypeStruct(vectors.shape, f32),
            jax.ShapeDtypeStruct((7, count), f32),
        ),
        in_specs=[kept] * 2,
        out_specs=(kept, kept),
        scratch_shapes=[dma((2,))],
        compiler_params=pltpu.CompilerParams(vmem_limit_bytes=1 << 20),
    )(*results)


def solution(mesh):
    spec4, spec3 = P(None, None, "tile", "col"), P(None, "tile", "col")
    return jax.shard_map(
        functools.partial(on_device, mesh.shape["col"], mesh.shape["tile"]),
        mesh=mesh,
        in_specs=(spec4, spec3, spec4, spec4, spec4),
        out_specs=(spec4, P()),
        check_vma=False,
    )
```

```python
import functools

import jax
import jax.numpy as jnp
from jax import lax
from jax.experimental import pallas as pl
from jax.experimental.pallas import tpu as pltpu
from jax.sharding import PartitionSpec as P

RIM = 2
BESIDE = [(0, 1), (0, -1), (1, 0), (-1, 0)]
LANES = 128
CODES = 18
MESH = pl.DeviceIdType.MESH
BONDS = ((0, 0), (-1, 0), (0, -1))
HOP, CODE, SITE, BOND2 = 4, 5, 6, 7


def relay_rounds(n_col, n_tile):
    rounds = [BESIDE]
    col, tile = 1, 1
    while col < n_col // 2 or tile < n_tile // 2:
        cols = (0, -col, col) if col < n_col // 2 else (0,)
        tiles = (0, -tile, tile) if tile < n_tile // 2 else (0,)
        rounds.append([(c, t) for c in cols for t in tiles if (c, t) != (0, 0)])
        col, tile = 2 * col, 2 * tile
    return rounds


def kernel(
    n_col, n_tile, orbitals,
    v_hbm, onsite_hbm, intra_hbm, index_hbm, hop_hbm,
    out_ref, mom_ref,
    v_ref, onsite_ref, intra_ref, index_ref, hop_ref, load_sem,
    area, term1, term2, term3, moved0, moved1, moved2, weights, weights_t, bond_t,
    packs, halo, sums, part, all_parts,
    row_send, row_recv, pack_send, pack_recv, part_send, part_recv, relay,
):
    rows = v_ref.shape[2]
    cols = v_ref.shape[3]
    blocks = cols // LANES
    ring = cols + LANES
    my_col = lax.axis_index("col")
    my_tile = lax.axis_index("tile")
    lane = lax.broadcasted_iota(jnp.int32, (8, LANES), 1)
    sub = lax.broadcasted_iota(jnp.int32, (8, LANES), 0)

    def col_at(step):
        return lax.rem(my_col + step + n_col, n_col)

    def tile_at(step):
        return lax.rem(my_tile + step + n_tile, n_tile)

    barrier = pltpu.get_barrier_semaphore()
    devices = n_col * n_tile
    me = my_col * n_tile + my_tile

    def device(step):
        at = lax.rem(me + step, devices)
        return (lax.div(at, n_tile), lax.rem(at, n_tile))

    def signal(semaphore, offsets):
        for c, t in offsets:
            pl.semaphore_signal(semaphore, inc=1, device_id=(col_at(c), tile_at(t)), device_id_type=MESH)

    signal(barrier, BESIDE)

    rounds = relay_rounds(n_col, n_tile)
    done = [0]

    def tell():
        if done[0] < len(rounds):
            signal(relay.at[done[0]], rounds[done[0]])

    def relay_on():
        if done[0] < len(rounds):
            pl.semaphore_wait(relay.at[done[0]], len(rounds[done[0]]))
            done[0] += 1
            tell()

    loads = [
        pltpu.make_async_copy(src, dst, load_sem.at[n])
        for n, (src, dst) in enumerate(
            (
                (v_hbm, v_ref),
                (hop_hbm, hop_ref),
                (index_hbm, index_ref),
                (onsite_hbm, onsite_ref),
                (intra_hbm, intra_ref),
            )
        )
    ]
    for load in loads:
        load.start()

    for load in loads:
        load.wait()
    own = slice(RIM, RIM + rows)
    for o in range(4):
        area[o, own, :, 0:cols] = jnp.swapaxes(v_ref[:, o], 0, 1)
    area[HOP, own, :, 0:cols] = jnp.swapaxes(hop_ref[...], 0, 1)
    area[CODE, own, :, 0:cols] = jnp.swapaxes(index_ref[...].astype(jnp.float32), 0, 1)
    area[SITE, own, :, 0:cols] = jnp.swapaxes(
        jnp.concatenate([onsite_ref[...], intra_ref[0:4]], axis=0), 0, 1
    )
    area[BOND2, own, :, 0:cols] = jnp.swapaxes(
        jnp.concatenate([intra_ref[4:6], jnp.zeros((6, rows, cols), jnp.float32)], axis=0), 0, 1
    )

    first, last, half = lane == 0, lane == LANES - 1, lane < LANES // 2
    slot_of = lane // 4
    terms = (term1, term2, term3)
    moved = (moved0, moved1, moved2)

    def block(b):
        return slice(b * LANES, (b + 1) * LANES)

    def pack(r, carry):
        out = list(carry)
        for g in range(8):
            i = (g % 4) * rows + r
            edges = jnp.where(half, area[g, RIM + r, :, 0:LANES], area[g, RIM + r, :, cols - LANES : cols])
            edges = pltpu.roll(edges, 4 * i, 1)
            out[g // 4] = jnp.where(slot_of == i, edges, out[g // 4])
            out[2 + g // 4] = jnp.where(
                slot_of == lax.rem(i + LANES // 4 - 1, LANES // 4), edges, out[2 + g // 4]
            )
        return tuple(out)

    zero = jnp.zeros((8, LANES), jnp.float32)
    packed = lax.fori_loop(0, rows, pack, (zero,) * 4)
    for n in range(4):
        packs[n // 2, n % 2] = packed[n]

    code_of = [(3 * sub + g).astype(jnp.float32) for g in range(3)]

    def weigh(r, s, b):
        at = block(b)
        total = [None] * 3
        for k in range(4):
            f = 2 * k + s
            code = jnp.broadcast_to(area[CODE, r, f : f + 1, at], (8, LANES))
            hop = jnp.broadcast_to(area[HOP, r, f : f + 1, at], (8, LANES))
            for g in range(3):
                x = jnp.where(code == code_of[g], hop, 0.0)
                total[g] = x if k == 0 else total[g] + x
        for g in range(3):
            weights[r, s, 8 * g : 8 * g + 8, at] = total[g]
        return total

    def back(x):
        return pltpu.roll(x, 1, 1)

    def ahead(x):
        return pltpu.roll(x, LANES - 1, 1)

    def loop(low, high, body):
        def step(i, carry):
            body(i)
            return carry

        lax.fori_loop(low, high, step, 0)

    low, high = RIM, RIM + rows
    def put(ref, at, b, x):
        ref[(*at, slice(None), block(b))] = x

    def own_turns(xs, way, store):
        if way < 0:
            ys = [back(x) for x in xs]
            for b in range(blocks):
                store(b, ys[b] if b == 0 else jnp.where(first, ys[b - 1], ys[b]))
        else:
            ys = [ahead(x) for x in xs]
            for b in range(blocks):
                store(b, ys[b] if b == blocks - 1 else jnp.where(last, ys[b + 1], ys[b]))

    def ring_turns(xs, way, store, count):
        if way < 0:
            ys = [back(x) for x in xs]
            for b in range(count):
                store(b, jnp.where(first, ys[b - 1], ys[b]))
        else:
            ys = [ahead(x) for x in xs]
            for b in range(count):
                store(b, jnp.where(last, ys[(b + 1) % (blocks + 1)], ys[b]))

    def edge_turns(x0, x3, x4, way, load, store):
        if way < 0:
            y3, y4 = back(x3), back(x4)
            store(0, jnp.where(first, y4, load(0)))
            store(blocks, jnp.where(first, y3, y4))
        else:
            y0, y4 = ahead(x0), ahead(x4)
            store(blocks - 1, jnp.where(last, y4, load(blocks - 1)))
            store(blocks, jnp.where(last, y0, y4))

    def field(g, r):
        return [area[g, r, :, block(b)] for b in range(blocks + 1)]

    def moved_at(ref, at):
        return lambda b, x: put(ref, at, b, x)

    def weights_at(r, s, g):
        def store(b, x):
            weights_t[r, s, 8 * g : 8 * g + 8, block(b)] = x
        return store

    def bond_at(r):
        def store(b, x):
            bond_t[r, :, block(b)] = x
        return store

    def prepare_own(r):
        for s in range(2):
            totals = [weigh(r, s, b) for b in range(blocks)]
            own_turns([t[0] for t in totals], 1, weights_at(r, s, 0))
            own_turns([t[2] for t in totals], -1, weights_at(r, s, 1))
        for o in range(4):
            xs = field(o, r)[:blocks]
            own_turns(xs, -1, moved_at(moved0, (0, o, r)))
            own_turns(xs, 1, moved_at(moved0, (1, o, r)))
        own_turns(field(BOND2, r)[:blocks], 1, bond_at(r))

    def unpack(r, theirs, dt, groups):
        for g in range(groups):
            i = (g % 4) * rows + theirs
            both = jnp.where(slot_of == i, halo[1 + dt, g // 4], halo[4 + dt, g // 4])
            area[g, r, :, cols:ring] = pltpu.roll(both, lax.rem(LANES - 4 * i, LANES), 1)

    def prepare_edges(r):
        unpack(r, r - low, 0, 8)
        b0, b3, b4 = block(0), block(blocks - 1), block(blocks)
        for s in range(2):
            total = weigh(r, s, blocks)
            for g, way in ((0, 1), (2, -1)):
                rows_of = slice(8 * g, 8 * g + 8)
                half_of = slice(4 * g, 4 * g + 8)
                edge_turns(
                    weights[r, s, rows_of, b0], weights[r, s, rows_of, b3], total[g], way,
                    lambda b, half_of=half_of, s=s: weights_t[r, s, half_of, block(b)],
                    weights_at(r, s, g // 2),
                )
        for o in range(4):
            x0, x3, x4 = area[o, r, :, b0], area[o, r, :, b3], area[o, r, :, b4]
            for side, way in ((0, -1), (1, 1)):
                edge_turns(
                    x0, x3, x4, way,
                    lambda b, o=o, side=side: moved0[side, o, r, :, block(b)],
                    moved_at(moved0, (side, o, r)),
                )
        edge_turns(
            area[BOND2, r, :, b0], None, area[BOND2, r, :, b4], 1,
            lambda b: bond_t[r, :, block(b)], bond_at(r),
        )

    def prepare(r, theirs, dt, groups):
        unpack(r, theirs, dt, groups)
        for s in range(2):
            totals = [weigh(r, s, b) for b in range(blocks + 1)]
            ring_turns([t[0] for t in totals], 1, weights_at(r, s, 0), blocks + 1)
            ring_turns([t[2] for t in totals], -1, weights_at(r, s, 1), blocks + 1)
        for o in range(4):
            xs = field(o, r)
            ring_turns(xs, -1, moved_at(moved0, (0, o, r)), blocks + 1)
            ring_turns(xs, 1, moved_at(moved0, (1, o, r)), blocks + 1)
        if groups == 8:
            ring_turns(field(BOND2, r), 1, bond_at(r), blocks + 1)

    for n in range(7):
        sums[n] = zero

    pl.semaphore_wait(barrier, len(BESIDE))
    tell()

    pack_copies = {}

    def send_packs(tiles):
        for side, step in ((0, -1), (1, 1)):
            for dt in tiles:
                slot = side * 3 + 1 - dt
                copy = pltpu.make_async_remote_copy(
                    src_ref=packs.at[side],
                    dst_ref=halo.at[slot],
                    send_sem=pack_send.at[slot],
                    recv_sem=pack_recv.at[slot],
                    device_id=(col_at(step), tile_at(dt)),
                    device_id_type=MESH,
                )
                copy.start()
                pack_copies[side, dt] = copy

    send_packs((0,))
    rim_copies = []

    def send_rim(layer, way, src, dst):
        copy = pltpu.make_async_remote_copy(
            src_ref=src,
            dst_ref=dst,
            send_sem=row_send.at[layer, way],
            recv_sem=row_recv.at[layer, way],
            device_id=(my_col, tile_at(1 - 2 * way)),
            device_id_type=MESH,
        )
        copy.start()
        rim_copies.append(copy)

    for layer in range(2):
        for way in range(2):
            src, dst = ((high - 1 - layer, low - 1 - layer), (low + layer, high + layer))[way]
            groups = 8 if layer == 0 else 6 + way
            send_rim(
                layer, way,
                area.at[0:groups, src : src + 1, :, 0:cols],
                area.at[0:groups, dst : dst + 1, :, 0:cols],
            )

    loop(low, high, prepare_own)
    relay_on()
    send_packs((-1, 1))

    def term(k, o, r, at):
        return area[o, r, :, at] if k == 0 else terms[k - 1][o, r, :, at]

    def hamiltonian(k, r, at):
        def v(o, row_off, col_off):
            if col_off == 0:
                return term(k, o, r + row_off, at)
            return moved[k][(col_off + 1) // 2, o, r + row_off, :, at]

        def spread(x):
            return jnp.broadcast_to(x, (8, LANES))

        def site(f, row):
            return spread(area[SITE, row, f : f + 1, at])

        outs = []
        for l in range(2):
            a, b = 2 * l, 2 * l + 1
            f0, f1 = site(4 + l, r), site(6 + l, r)
            f2 = spread(area[BOND2, r, l : l + 1, at])
            outs.append(
                site(a, r) * v(a, 0, 0) + f0 * v(b, 0, 0) + f1 * v(b, -1, 0) + f2 * v(b, 0, -1)
            )
            outs.append(
                site(b, r) * v(b, 0, 0)
                + f0 * v(a, 0, 0)
                + site(6 + l, r + 1) * v(a, 1, 0)
                + spread(bond_t[r, l : l + 1, at]) * v(a, 0, 1)
            )
        for s in range(2):
            for c in range(CODES):
                t, e, f = c // 9, c % 9 // 3 - 1, c % 3 - 1
                n = 8 * (f + 1) + 3 * t + e + 1
                outs[s] = outs[s] + spread(weights[r, s, n : n + 1, at]) * v(2 + t, e, f)
                if f == 0:
                    other = weights[r - e, s, n : n + 1, at]
                else:
                    n = 4 * (f + 1) + 3 * t + e + 1
                    other = weights_t[r - e, s, n : n + 1, at]
                outs[2 + t] = outs[2 + t] + spread(other) * v(s, -e, -f)
        return outs

    def advance(k, r):
        inside = jnp.where((r >= RIM) & (r < RIM + rows), 1.0, 0.0).astype(jnp.float32)
        cross, square, first_sum = zero, zero, zero
        turns = [{} for _ in range(4)]

        def store_turn(o, way, b):
            near, far = turns[o][b], turns[o][(b + way) % (blocks + 1)]
            if way < 0:
                x = jnp.where(first, far[0], near[0])
            else:
                x = jnp.where(last, far[1], near[1])
            moved[k + 1][(way + 1) // 2, o, r, :, block(b)] = x

        for b in ([blocks] if k < 2 else []) + list(range(blocks)):
            at = block(b)
            outs = hamiltonian(k, r, at)
            for o in range(4):
                old = term(k, o, r, at)
                new = outs[o] if k == 0 else 2.0 * outs[o] - term(k - 1, o, r, at)
                terms[k][o, r, :, at] = new
                if b < blocks:
                    cross = cross + new * old
                    square = square + new * new
                    if k == 0:
                        first_sum = first_sum + old * old
                if k < 2:
                    turns[o][b] = (back(new), ahead(new))
                    if b < blocks:
                        store_turn(o, -1, b)
                    if 0 < b < blocks:
                        store_turn(o, 1, b - 1)
                    if b == 0 and k == 0:
                        store_turn(o, 1, blocks)
        if k < 2:
            for o in range(4):
                store_turn(o, 1, blocks - 1)
                if k == 0:
                    store_turn(o, -1, blocks)
        if k == 0:
            sums[0] += inside * first_sum
        sums[2 * k + 1] += inside * cross
        sums[2 * k + 2] += inside * square

    for side in range(2):
        pack_copies[side, 0].wait_recv()
    loop(low, high, prepare_edges)
    loop(0, 2, lambda i: advance(0, low + 1 + i * (rows - 3)))
    send_rim(2, 0, term1.at[:, high - 2 : high - 1], term1.at[:, 0:1])
    send_rim(2, 1, term1.at[:, low + 1 : low + 2], term1.at[:, high + 1 : high + 2])
    loop(low + 2, high - 2, functools.partial(advance, 0))
    relay_on()
    for k in (1, 2):
        loop(low + 1 + k, high - 1 - k, functools.partial(advance, k))

    for side in range(2):
        for dt in (-1, 1):
            pack_copies[side, dt].wait_recv()
    for layer in range(3):
        for way in range(2):
            rim_copies[2 * layer + way].wait_recv()
        if layer < 2:
            prepare(low - 1 - layer, rows - 1 - layer, -1, 8 if layer == 0 else 6)
            prepare(high + layer, layer, 1, 8 if layer == 0 else 7)
        else:
            for r in (0, high + 1):
                for o in range(4):
                    xs = [term1[o, r, :, block(b)] for b in range(blocks + 1)]
                    ring_turns(xs, -1, moved_at(moved1, (0, o, r)), blocks + 1)
                    ring_turns(xs, 1, moved_at(moved1, (1, o, r)), blocks + 1)
        for k in range(1 if layer == 2 else 0, 3):
            top, bottom = low - layer + k, high - 1 + layer - k
            loop(0, 2, lambda i, k=k: advance(k, top + i * (bottom - top)))
        relay_on()

    row = jnp.zeros((8, LANES), jnp.float32)
    for n in range(7):
        total = jnp.sum(sums[n], axis=1, keepdims=True)
        row = jnp.where(lane == sub + 8 * n, jnp.broadcast_to(total, (8, LANES)), row)
    part[...] = jnp.sum(row, axis=0, keepdims=True)
    all_parts[me] = part[...]

    def other(step):
        at = jnp.where(step > me, step, step - 1)
        return (lax.div(at, n_tile), lax.rem(at, n_tile))

    def part_copy(step):
        return pltpu.make_async_remote_copy(
            src_ref=part,
            dst_ref=all_parts.at[me],
            send_sem=part_send,
            recv_sem=part_recv,
            device_id=other(step),
            device_id_type=MESH,
        )

    while done[0] < len(rounds):
        relay_on()
    loop(1, devices, lambda i: part_copy(i).start())
    for o in range(4):
        out_ref[:, o] = jnp.swapaxes(term3[o, own, :, 0:cols], 0, 1)

    for copy in rim_copies + list(pack_copies.values()):
        copy.wait_send()
    arrived = pltpu.make_async_remote_copy(
        src_ref=all_parts.at[1:devices],
        dst_ref=all_parts.at[1:devices],
        send_sem=part_send,
        recv_sem=part_recv,
        device_id=device(1),
        device_id_type=MESH,
    )
    arrived.wait_recv()
    arrived.wait_send()
    pieces = [all_parts[n] for n in range(devices)]
    while len(pieces) > 1:
        half_way = (len(pieces) + 1) // 2
        pieces = [
            pieces[n] + pieces[n + half_way] if n + half_way < len(pieces) else pieces[n]
            for n in range(half_way)
        ]
    total = pieces[0]
    total = jnp.broadcast_to(total / orbitals, (8, LANES))
    scaled = [pltpu.roll(total, (LANES - 8 * n) % LANES, 1)[0:1, 0:8] for n in range(7)]
    mom_ref[0:1, :] = scaled[0]
    mom_ref[1:2, :] = scaled[1]
    for n in range(2, 7):
        mom_ref[n : n + 1, :] = 2.0 * scaled[n] - scaled[n % 2]


def emit(last_ref, rows_ref, out_ref, mom_ref, sem):
    copies = [
        pltpu.make_async_copy(last_ref, out_ref, sem.at[0]),
        pltpu.make_async_copy(rows_ref, mom_ref, sem.at[1]),
    ]
    for copy in copies:
        copy.start()
    for copy in copies:
        copy.wait()


def on_device(n_col, n_tile, vectors, onsite, intra_hop, inter_index, inter_hop):
    count, _, rows, cols = vectors.shape
    slots = inter_index.shape[0]
    assert n_col > 2 and n_tile > 2
    assert count == 8 and slots == 4 and rows == 8 and cols % LANES == 0
    tall = rows + 2 * RIM
    ring = cols + LANES
    f32 = jnp.float32
    vmem = pl.BlockSpec(memory_space=pltpu.VMEM)
    dma = pltpu.SemaphoreType.DMA
    results = pl.pallas_call(
        functools.partial(kernel, n_col, n_tile, 4 * rows * cols * n_col * n_tile),
        out_shape=(
            jax.ShapeDtypeStruct(vectors.shape, f32),
            jax.ShapeDtypeStruct((7, count), f32),
        ),
        in_specs=[pl.BlockSpec(memory_space=pltpu.HBM)] * 5,
        out_specs=(vmem, vmem),
        scratch_shapes=[
            pltpu.VMEM(vectors.shape, f32),
            pltpu.VMEM(onsite.shape, f32),
            pltpu.VMEM((6, rows, cols), f32),
            pltpu.VMEM((2 * slots, rows, cols), jnp.int32),
            pltpu.VMEM((2 * slots, rows, cols), f32),
            dma((5,)),
            pltpu.VMEM((8, tall, 8, ring), f32),
            *[pltpu.VMEM((4, tall, 8, ring), f32)] * 3,
            *[pltpu.VMEM((2, 4, tall, 8, ring), f32)] * 3,
            pltpu.VMEM((tall, 2, 24, ring), f32),
            pltpu.VMEM((tall, 2, 16, ring), f32),
            pltpu.VMEM((tall, 8, ring), f32),
            pltpu.VMEM((2, 2, 8, LANES), f32),
            pltpu.VMEM((6, 2, 8, LANES), f32),
            pltpu.VMEM((7, 8, LANES), f32),
            pltpu.VMEM((1, LANES), f32),
            pltpu.VMEM((n_col * n_tile, 1, LANES), f32),
            dma((3, 2)), dma((3, 2)), dma((6,)), dma((6,)), dma, dma,
            pltpu.SemaphoreType.REGULAR((len(relay_rounds(n_col, n_tile)),)),
        ],
        compiler_params=pltpu.CompilerParams(
            collective_id=0, has_side_effects=True, vmem_limit_bytes=32 << 20
        ),
    )(
        *(
            pltpu.with_memory_space_constraint(x, pltpu.HBM)
            for x in (
                vectors,
                onsite,
                intra_hop.reshape(6, rows, cols),
                inter_index.reshape(2 * slots, rows, cols),
                inter_hop.reshape(2 * slots, rows, cols),
            )
        )
    )
    kept = pl.BlockSpec(memory_space=pl.ANY)
    return pl.pallas_call(
        emit,
        out_shape=(
            jax.ShapeDtypeStruct(vectors.shape, f32),
            jax.ShapeDtypeStruct((7, count), f32),
        ),
        in_specs=[kept] * 2,
        out_specs=(kept, kept),
        scratch_shapes=[dma((2,))],
        compiler_params=pltpu.CompilerParams(vmem_limit_bytes=1 << 20),
    )(*results)


def solution(mesh):
    spec4, spec3 = P(None, None, "tile", "col"), P(None, "tile", "col")
    return jax.shard_map(
        functools.partial(on_device, mesh.shape["col"], mesh.shape["tile"]),
        mesh=mesh,
        in_specs=(spec4, spec3, spec4, spec4, spec4),
        out_specs=(spec4, P()),
        check_vma=False,
    )
```

```python
import functools

import jax
import jax.numpy as jnp
from jax import lax
from jax.experimental import pallas as pl
from jax.experimental.pallas import tpu as pltpu
from jax.sharding import PartitionSpec as P

RIM = 2
STEPS = 3
WIDE = 3 * STEPS
BESIDE = [(0, 1), (0, -1), (1, 0), (-1, 0)]
LANES = 128
CODES = 18
MESH = pl.DeviceIdType.MESH
BONDS = ((0, 0), (-1, 0), (0, -1))
HOP, CODE, SITE, BOND2 = 4, 5, 6, 7


def relay_rounds(n_col, n_tile):
    rounds = [BESIDE]
    col, tile = 1, 1
    while col < n_col // 2 or tile < n_tile // 2:
        cols = (0, -col, col) if col < n_col // 2 else (0,)
        tiles = (0, -tile, tile) if tile < n_tile // 2 else (0,)
        rounds.append([(c, t) for c in cols for t in tiles if (c, t) != (0, 0)])
        col, tile = 2 * col, 2 * tile
    return rounds


def kernel(
    n_col, n_tile, orbitals,
    v_hbm, onsite_hbm, intra_hbm, index_hbm, hop_hbm,
    out_ref, mom_ref,
    v_ref, onsite_ref, intra_ref, index_ref, hop_ref, load_sem,
    area, term1, term2, term3, moved0, moved1, moved2, weights, weights_t, bond_t,
    packs, halo, tile_packs, tile_halo, strips, strip_site, strip_weights, sums, part, all_parts,
    row_send, row_recv, pack_send, pack_recv, tile_send, tile_recv, part_send, part_recv, relay,
):
    rows = v_ref.shape[2]
    cols = v_ref.shape[3]
    blocks = cols // LANES
    ring = cols
    my_col = lax.axis_index("col")
    my_tile = lax.axis_index("tile")
    lane = lax.broadcasted_iota(jnp.int32, (8, LANES), 1)
    sub = lax.broadcasted_iota(jnp.int32, (8, LANES), 0)

    def col_at(step):
        return lax.rem(my_col + step + n_col, n_col)

    def tile_at(step):
        return lax.rem(my_tile + step + n_tile, n_tile)

    barrier = pltpu.get_barrier_semaphore()
    devices = n_col * n_tile
    me = my_col * n_tile + my_tile

    def device(step):
        at = lax.rem(me + step, devices)
        return (lax.div(at, n_tile), lax.rem(at, n_tile))

    def signal(semaphore, offsets):
        for c, t in offsets:
            pl.semaphore_signal(semaphore, inc=1, device_id=(col_at(c), tile_at(t)), device_id_type=MESH)

    signal(barrier, BESIDE)

    rounds = relay_rounds(n_col, n_tile)
    done = [0]

    def tell():
        if done[0] < len(rounds):
            signal(relay.at[done[0]], rounds[done[0]])

    def relay_on():
        if done[0] < len(rounds):
            pl.semaphore_wait(relay.at[done[0]], len(rounds[done[0]]))
            done[0] += 1
            tell()

    loads = [
        pltpu.make_async_copy(src, dst, load_sem.at[n])
        for n, (src, dst) in enumerate(
            (
                (v_hbm, v_ref),
                (hop_hbm, hop_ref),
                (index_hbm, index_ref),
                (onsite_hbm, onsite_ref),
                (intra_hbm, intra_ref),
            )
        )
    ]
    for load in loads:
        load.start()

    for load in loads:
        load.wait()
    own = slice(RIM, RIM + rows)
    for o in range(4):
        area[o, own, :, 0:cols] = jnp.swapaxes(v_ref[:, o], 0, 1)
    area[HOP, own, :, 0:cols] = jnp.swapaxes(hop_ref[...], 0, 1)
    area[CODE, own, :, 0:cols] = jnp.swapaxes(index_ref[...].astype(jnp.float32), 0, 1)
    area[SITE, own, :, 0:cols] = jnp.swapaxes(
        jnp.concatenate([onsite_ref[...], intra_ref[0:4]], axis=0), 0, 1
    )
    area[BOND2, own, :, 0:cols] = jnp.swapaxes(
        jnp.concatenate(
            [intra_ref[4:6], pltpu.roll(intra_ref[2:4], rows - 1, 1), jnp.zeros((4, rows, cols), jnp.float32)], axis=0
        ),
        0,
        1,
    )

    first, last, half = lane == 0, lane == LANES - 1, lane < LANES // 2
    terms = (term1, term2, term3)
    moved = (moved0, moved1, moved2)

    def block(b):
        return slice(b * LANES, (b + 1) * LANES)

    zero = jnp.zeros((8, LANES), jnp.float32)

    def shift(x, by):
        by = by % LANES
        return pltpu.roll(x, by, 1) if by else x

    def over(x):
        return functools.reduce(jnp.add, [jnp.where(x >= WIDE * n, 1, 0) for n in range(1, LANES // WIDE + 1)])

    turned = jnp.where(lane >= LANES - STEPS, lane - (LANES - STEPS), lane + STEPS)
    strip_row = [over(lane), over(turned)]
    within = lane - WIDE * strip_row[0]
    strip_col = [within, turned - WIDE * strip_row[1]]
    lefts, mids = within < STEPS, (within >= STEPS) & (within < 2 * STEPS)
    own_cols = [strip_col[0] >= STEPS, strip_col[1] < 2 * STEPS]
    above = [strip_row[n] < STEPS for n in range(2)]
    below = [strip_row[n] >= STEPS + rows for n in range(2)]

    def build_strips():
        for g in range(8):
            kept = [zero, zero]
            for i in range(rows):
                edges = jnp.where(half, area[g, RIM + i, :, 0:LANES], area[g, RIM + i, :, cols - LANES : cols])
                edges = shift(edges, WIDE * (i + STEPS) + STEPS)
                for n in range(2):
                    kept[n] = jnp.where((strip_row[n] == i + STEPS) & own_cols[n], edges, kept[n])
            for n in range(2):
                strips[n, g] = kept[n]
        for n in range(3):
            for side in range(2):
                x = strips[side, 3 * n]
                y = shift(strips[side, 3 * n + 1], STEPS)
                z = strips[side, 3 * n + 2] if n < 2 else zero
                z = shift(z, -STEPS if side == 0 else 2 * STEPS)
                if side == 0:
                    packs[side, n] = jnp.where(lefts, z, jnp.where(mids, x, y))
                else:
                    packs[side, n] = jnp.where(lefts, x, jnp.where(mids, y, z))

    def build_tile_packs():
        for way in range(2):
            start = WIDE * (rows if way == 0 else STEPS)
            for n in range(4):
                x = zero
                for j in range(4):
                    side, g = (4 * n + j) // 8, (4 * n + j) % 8
                    y = shift(strips[side, g], 32 * j - start + STEPS * side)
                    x = jnp.where(lane // 32 == j, y, x)
                tile_packs[way, n] = x

    code_of = [(3 * sub + g).astype(jnp.float32) for g in range(3)]

    def weigh_of(codes, hops, s):
        total = [None] * 3
        for k in range(4):
            f = 2 * k + s
            code = jnp.broadcast_to(codes(f), (8, LANES))
            hop = jnp.broadcast_to(hops(f), (8, LANES))
            for g in range(3):
                x = jnp.where(code == code_of[g], hop, 0.0)
                total[g] = x if k == 0 else total[g] + x
        return total

    def weigh(r, s, b):
        at = block(b)
        total = weigh_of(lambda f: area[CODE, r, f : f + 1, at], lambda f: area[HOP, r, f : f + 1, at], s)
        for g in range(3):
            weights[r, s, 8 * g : 8 * g + 8, at] = total[g]
        return total

    def back(x):
        return pltpu.roll(x, 1, 1)

    def ahead(x):
        return pltpu.roll(x, LANES - 1, 1)

    def loop(low, high, body):
        def step(i, carry):
            body(i)
            return carry

        lax.fori_loop(low, high, step, 0)

    low, high = RIM, RIM + rows
    def put(ref, at, b, x):
        ref[(*at, slice(None), block(b))] = x

    def own_turns(xs, way, store):
        if way < 0:
            ys = [back(x) for x in xs]
            for b in range(blocks):
                store(b, ys[b] if b == 0 else jnp.where(first, ys[b - 1], ys[b]))
        else:
            ys = [ahead(x) for x in xs]
            for b in range(blocks):
                store(b, ys[b] if b == blocks - 1 else jnp.where(last, ys[b + 1], ys[b]))

    def field(g, r):
        return [area[g, r, :, block(b)] for b in range(blocks)]

    def moved_at(ref, at):
        return lambda b, x: put(ref, at, b, x)

    def weights_at(r, s, g):
        def store(b, x):
            weights_t[r, s, 8 * g : 8 * g + 8, block(b)] = x
        return store

    def bond_at(r):
        def store(b, x):
            bond_t[r, :, block(b)] = x
        return store

    def prepare(r, bonds=True):
        for s in range(2):
            totals = [weigh(r, s, b) for b in range(blocks)]
            own_turns([t[0] for t in totals], 1, weights_at(r, s, 0))
            own_turns([t[2] for t in totals], -1, weights_at(r, s, 1))
        for o in range(4):
            xs = field(o, r)
            own_turns(xs, -1, moved_at(moved0, (0, o, r)))
            own_turns(xs, 1, moved_at(moved0, (1, o, r)))
        if bonds:
            own_turns(field(BOND2, r), 1, bond_at(r))

    for n in range(7):
        sums[n] = zero

    pl.semaphore_wait(barrier, len(BESIDE))
    tell()

    near = lax.rem(my_tile, 2)
    far = 1 - near

    def edge(way):
        return jnp.where(way == 0, low, high - 1), 2 * way - 1

    def rim(layer, way):
        deep = 1 if layer == 2 else layer
        src = jnp.where(way == 0, high - 1 - deep, low + deep)
        row, out = edge(way)
        dst = row + out * (min(layer, 1) + 1)
        if layer == 2:
            src_ref, dst_ref = term1.at[:, pl.ds(src, 1)], term1.at[:, pl.ds(dst, 1)]
        else:
            groups = 8 if layer == 0 else 6
            src_ref = area.at[0:groups, pl.ds(src, 1), :, 0:cols]
            dst_ref = area.at[0:groups, pl.ds(dst, 1), :, 0:cols]
        return pltpu.make_async_remote_copy(
            src_ref=src_ref,
            dst_ref=dst_ref,
            send_sem=row_send.at[layer, way],
            recv_sem=row_recv.at[layer, way],
            device_id=(my_col, tile_at(1 - 2 * way)),
            device_id_type=MESH,
        )

    for layer, away in ((0, 1), (0, 0), (1, 1), (1, 0)):
        rim(layer, far if away else near).start()

    pack_copies = {}

    def send_packs(tiles):
        for side, step in ((0, -1), (1, 1)):
            for dt in tiles:
                slot = side * 3 + 1 - dt
                copy = pltpu.make_async_remote_copy(
                    src_ref=packs.at[side],
                    dst_ref=halo.at[slot],
                    send_sem=pack_send.at[slot],
                    recv_sem=pack_recv.at[slot],
                    device_id=(col_at(step), tile_at(dt)),
                    device_id_type=MESH,
                )
                copy.start()
                pack_copies[side, dt] = copy

    build_strips()
    send_packs((0,))
    build_tile_packs()
    tile_copies = []
    for way in range(2):
        copy = pltpu.make_async_remote_copy(
            src_ref=tile_packs.at[way],
            dst_ref=tile_halo.at[way],
            send_sem=tile_send.at[way],
            recv_sem=tile_recv.at[way],
            device_id=(my_col, tile_at(1 - 2 * way)),
            device_id_type=MESH,
        )
        copy.start()
        tile_copies.append(copy)

    loop(low, high, prepare)
    relay_on()
    send_packs((-1, 1))

    def term(k, o, r, at):
        return area[o, r, :, at] if k == 0 else terms[k - 1][o, r, :, at]

    def hamiltonian(k, r, at):
        def v(o, row_off, col_off):
            if col_off == 0:
                return term(k, o, r + row_off, at)
            return moved[k][(col_off + 1) // 2, o, r + row_off, :, at]

        def spread(x):
            return jnp.broadcast_to(x, (8, LANES))

        def site(f, row):
            return spread(area[SITE, row, f : f + 1, at])

        outs = []
        for l in range(2):
            a, b = 2 * l, 2 * l + 1
            f0, f1 = site(4 + l, r), site(6 + l, r)
            f2 = spread(area[BOND2, r, l : l + 1, at])
            outs.append(
                site(a, r) * v(a, 0, 0) + f0 * v(b, 0, 0) + f1 * v(b, -1, 0) + f2 * v(b, 0, -1)
            )
            outs.append(
                site(b, r) * v(b, 0, 0)
                + f0 * v(a, 0, 0)
                + site(6 + l, r + 1) * v(a, 1, 0)
                + spread(bond_t[r, l : l + 1, at]) * v(a, 0, 1)
            )
        for s in range(2):
            for c in range(CODES):
                t, e, f = c // 9, c % 9 // 3 - 1, c % 3 - 1
                n = 8 * (f + 1) + 3 * t + e + 1
                outs[s] = outs[s] + spread(weights[r, s, n : n + 1, at]) * v(2 + t, e, f)
                if f == 0:
                    other = weights[r - e, s, n : n + 1, at]
                else:
                    n = 4 * (f + 1) + 3 * t + e + 1
                    other = weights_t[r - e, s, n : n + 1, at]
                outs[2 + t] = outs[2 + t] + spread(other) * v(s, -e, -f)
        return outs

    def advance(k, r):
        inside = jnp.where((r >= RIM) & (r < RIM + rows), 1.0, 0.0).astype(jnp.float32)
        cross, square, first_sum = zero, zero, zero
        turns = [{} for _ in range(4)]

        def store_turn(o, way, b):
            near = turns[o][b][(way + 1) // 2]
            if 0 <= b + way < blocks:
                near = jnp.where(first if way < 0 else last, turns[o][b + way][(way + 1) // 2], near)
            moved[k + 1][(way + 1) // 2, o, r, :, block(b)] = near

        for b in range(blocks):
            at = block(b)
            outs = hamiltonian(k, r, at)
            crosses, squares = zero, zero
            for o in range(4):
                old = term(k, o, r, at)
                new = outs[o] if k == 0 else 2.0 * outs[o] - term(k - 1, o, r, at)
                terms[k][o, r, :, at] = new
                crosses = crosses + new * old
                squares = squares + new * new
                if k == 0:
                    first_sum = first_sum + old * old
                if k < 2:
                    turns[o][b] = (back(new), ahead(new))
                    store_turn(o, -1, b)
                    if b > 0:
                        store_turn(o, 1, b - 1)
            if b == 0:
                crosses, squares = (jnp.where(lane > k, x, 0.0) for x in (crosses, squares))
            if b == blocks - 1:
                crosses, squares = (jnp.where(lane < LANES - 1 - k, x, 0.0) for x in (crosses, squares))
            cross, square = cross + crosses, square + squares
        if k < 2:
            for o in range(4):
                store_turn(o, 1, blocks - 1)
        if k == 0:
            sums[0] += inside * first_sum
        sums[2 * k + 1] += inside * cross
        sums[2 * k + 2] += inside * square

    def strip_terms(n):
        sides = [
            [halo[3 * (1 - n) + m, i] for i in range(3)] for m in range(3)
        ]
        side = [
            jnp.where(
                above[0], shift(sides[0][i], -WIDE * rows), jnp.where(below[0], shift(sides[2][i], WIDE * rows), sides[1][i])
            )
            for i in range(3)
        ]
        turns = (0, -STEPS, -2 * STEPS) if n == 0 else (0, -STEPS, STEPS)
        fields = []
        for g in range(8):
            m, j = divmod(8 * n + g, 4)
            top = shift(tile_halo[0, m], -32 * j - STEPS * n)
            bottom = shift(tile_halo[1, m], WIDE * (STEPS + rows) - 32 * j - STEPS * n)
            x = jnp.where(above[n], top, jnp.where(below[n], bottom, strips[n, g]))
            fields.append(jnp.where(mids if n else lefts, shift(side[g // 3], turns[g % 3]), x))
        strip_site[n, 0], strip_site[n, 1] = fields[SITE], fields[BOND2]
        strips[n, HOP], strips[n, CODE] = fields[HOP], fields[CODE]
        for s in range(2):
            totals = weigh_of(lambda f: strips[n, CODE, f : f + 1], lambda f: strips[n, HOP, f : f + 1], s)
            for g in range(3):
                strip_weights[n, s, 8 * g : 8 * g + 8] = totals[g]

        def spread(x):
            return jnp.broadcast_to(x, (8, LANES))

        def at(x, e, f):
            return shift(x, -(WIDE * e + f))

        def apply(v):
            outs = [None] * 4
            for l in range(2):
                a, b = 2 * l, 2 * l + 1
                sa, sb, f0, f1 = (spread(strip_site[n, 0, i : i + 1]) for i in (a, b, 4 + l, 6 + l))
                f2 = spread(strip_site[n, 1, l : l + 1])
                outs[a] = sa * v[a] + f0 * v[b] + f1 * at(v[b], -1, 0) + f2 * at(v[b], 0, -1)
                outs[b] = sb * v[b] + f0 * v[a] + at(f1 * v[a], 1, 0) + at(f2 * v[a], 0, 1)
            for c in range(CODES):
                t, e, f = c // 9, c % 9 // 3 - 1, c % 3 - 1
                i = 8 * (f + 1) + 3 * t + e + 1
                w = [spread(strip_weights[n, s, i : i + 1]) for s in range(2)]
                far = at(v[2 + t], e, f)
                for s in range(2):
                    outs[s] = outs[s] + w[s] * far
                outs[2 + t] = outs[2 + t] + at(w[0] * v[0] + w[1] * v[1], -e, -f)
            return outs

        older, old = None, fields[0:4]
        for k in range(3):
            outs = apply(old)
            new = outs if k == 0 else [2.0 * outs[o] - older[o] for o in range(4)]
            col = strip_col[n] - (STEPS if n == 0 else 0)
            wanted = (col >= 0) & (col <= k) if n == 0 else (col >= 5 - k) & (col <= 5)
            wanted = wanted & ~above[n] & ~below[n]
            cross = functools.reduce(jnp.add, [new[o] * old[o] for o in range(4)])
            square = functools.reduce(jnp.add, [new[o] * new[o] for o in range(4)])
            sums[2 * k + 1] += jnp.where(wanted, cross, 0.0)
            sums[2 * k + 2] += jnp.where(wanted, square, 0.0)
            older, old = old, new
        for o in range(4):
            strips[n, o] = old[o]

    loop(0, 2, lambda i: advance(0, low + 1 + i * (rows - 3)))
    rim(2, far).start()
    rim(2, near).start()
    loop(low + 2, high - 2, functools.partial(advance, 0))
    relay_on()
    for k in (1, 2):
        loop(low + 1 + k, high - 1 - k, functools.partial(advance, k))

    def rims(i):
        way = jnp.where(i == 0, far, near)
        row, out = edge(way)
        for layer in range(3):
            rim(layer, way).wait_recv()
            r = row + out * (min(layer, 1) + 1)
            if layer < 2:
                prepare(r, layer == 0)
                if layer == 0:
                    area[SITE, r + out, 6:8, :] = area[BOND2, r, 2:4, :]
            else:
                for o in range(4):
                    xs = [term1[o, r, :, block(b)] for b in range(blocks)]
                    own_turns(xs, -1, moved_at(moved1, (0, o, r)))
                    own_turns(xs, 1, moved_at(moved1, (1, o, r)))
            for k in range(1 if layer == 2 else 0, 3):
                advance(k, row + out * (layer - k))

    loop(0, 2, rims)
    for copy in pack_copies.values():
        copy.wait_recv()
    for copy in tile_copies:
        copy.wait_recv()
    for n in range(2):
        strip_terms(n)

    row = jnp.zeros((8, LANES), jnp.float32)
    for n in range(7):
        total = jnp.sum(sums[n], axis=1, keepdims=True)
        row = jnp.where(lane == sub + 8 * n, jnp.broadcast_to(total, (8, LANES)), row)
    part[...] = jnp.sum(row, axis=0, keepdims=True)
    all_parts[me] = part[...]

    def other(step):
        at = jnp.where(step > me, step, step - 1)
        return (lax.div(at, n_tile), lax.rem(at, n_tile))

    def part_copy(step):
        return pltpu.make_async_remote_copy(
            src_ref=part,
            dst_ref=all_parts.at[me],
            send_sem=part_send,
            recv_sem=part_recv,
            device_id=other(step),
            device_id_type=MESH,
        )

    while done[0] < len(rounds):
        relay_on()
    loop(1, devices, lambda i: part_copy(i).start())
    for o in range(4):
        both = jnp.where(lefts, strips[1, o], strips[0, o])
        for i in range(rows):
            x = shift(both, -(WIDE * (i + STEPS) + STEPS))
            term3[o, low + i, :, 0:LANES] = jnp.where(lane < STEPS, x, term3[o, low + i, :, 0:LANES])
            edge_at = slice(cols - LANES, cols)
            term3[o, low + i, :, edge_at] = jnp.where(lane >= LANES - STEPS, x, term3[o, low + i, :, edge_at])
    for o in range(4):
        out_ref[:, o] = jnp.swapaxes(term3[o, own, :, 0:cols], 0, 1)

    for copy in (*pack_copies.values(), *tile_copies):
        copy.wait_send()
    for layer in range(3):
        for way in range(2):
            rim(layer, way).wait_send()
    arrived = pltpu.make_async_remote_copy(
        src_ref=all_parts.at[1:devices],
        dst_ref=all_parts.at[1:devices],
        send_sem=part_send,
        recv_sem=part_recv,
        device_id=device(1),
        device_id_type=MESH,
    )
    arrived.wait_recv()
    arrived.wait_send()
    pieces = [all_parts[n] for n in range(devices)]
    while len(pieces) > 1:
        half_way = (len(pieces) + 1) // 2
        pieces = [
            pieces[n] + pieces[n + half_way] if n + half_way < len(pieces) else pieces[n]
            for n in range(half_way)
        ]
    total = pieces[0]
    total = jnp.broadcast_to(total / orbitals, (8, LANES))
    scaled = [pltpu.roll(total, (LANES - 8 * n) % LANES, 1)[0:1, 0:8] for n in range(7)]
    mom_ref[0:1, :] = scaled[0]
    mom_ref[1:2, :] = scaled[1]
    for n in range(2, 7):
        mom_ref[n : n + 1, :] = 2.0 * scaled[n] - scaled[n % 2]


def emit(last_ref, rows_ref, out_ref, mom_ref, sem):
    copies = [
        pltpu.make_async_copy(last_ref, out_ref, sem.at[0]),
        pltpu.make_async_copy(rows_ref, mom_ref, sem.at[1]),
    ]
    for copy in copies:
        copy.start()
    for copy in copies:
        copy.wait()


def on_device(n_col, n_tile, vectors, onsite, intra_hop, inter_index, inter_hop):
    count, _, rows, cols = vectors.shape
    slots = inter_index.shape[0]
    assert n_col > 2 and n_tile > 2
    assert count == 8 and slots == 4 and rows == 8 and cols % LANES == 0
    tall = rows + 2 * RIM
    ring = cols
    f32 = jnp.float32
    vmem = pl.BlockSpec(memory_space=pltpu.VMEM)
    dma = pltpu.SemaphoreType.DMA
    results = pl.pallas_call(
        functools.partial(kernel, n_col, n_tile, 4 * rows * cols * n_col * n_tile),
        out_shape=(
            jax.ShapeDtypeStruct(vectors.shape, f32),
            jax.ShapeDtypeStruct((7, count), f32),
        ),
        in_specs=[pl.BlockSpec(memory_space=pltpu.HBM)] * 5,
        out_specs=(vmem, vmem),
        scratch_shapes=[
            pltpu.VMEM(vectors.shape, f32),
            pltpu.VMEM(onsite.shape, f32),
            pltpu.VMEM((6, rows, cols), f32),
            pltpu.VMEM((2 * slots, rows, cols), jnp.int32),
            pltpu.VMEM((2 * slots, rows, cols), f32),
            dma((5,)),
            pltpu.VMEM((8, tall, 8, ring), f32),
            *[pltpu.VMEM((4, tall, 8, ring), f32)] * 3,
            *[pltpu.VMEM((2, 4, tall, 8, ring), f32)] * 3,
            pltpu.VMEM((tall, 2, 24, ring), f32),
            pltpu.VMEM((tall, 2, 16, ring), f32),
            pltpu.VMEM((tall, 8, ring), f32),
            pltpu.VMEM((2, 3, 8, LANES), f32),
            pltpu.VMEM((6, 3, 8, LANES), f32),
            pltpu.VMEM((2, 4, 8, LANES), f32),
            pltpu.VMEM((2, 4, 8, LANES), f32),
            pltpu.VMEM((2, 8, 8, LANES), f32),
            pltpu.VMEM((2, 2, 8, LANES), f32),
            pltpu.VMEM((2, 2, 24, LANES), f32),
            pltpu.VMEM((7, 8, LANES), f32),
            pltpu.VMEM((1, LANES), f32),
            pltpu.VMEM((n_col * n_tile, 1, LANES), f32),
            dma((3, 2)), dma((3, 2)), dma((6,)), dma((6,)), dma((2,)), dma((2,)), dma, dma,
            pltpu.SemaphoreType.REGULAR((len(relay_rounds(n_col, n_tile)),)),
        ],
        compiler_params=pltpu.CompilerParams(
            collective_id=0, has_side_effects=True, vmem_limit_bytes=32 << 20
        ),
    )(
        *(
            pltpu.with_memory_space_constraint(x, pltpu.HBM)
            for x in (
                vectors,
                onsite,
                intra_hop.reshape(6, rows, cols),
                inter_index.reshape(2 * slots, rows, cols),
                inter_hop.reshape(2 * slots, rows, cols),
            )
        )
    )
    kept = pl.BlockSpec(memory_space=pl.ANY)
    return pl.pallas_call(
        emit,
        out_shape=(
            jax.ShapeDtypeStruct(vectors.shape, f32),
            jax.ShapeDtypeStruct((7, count), f32),
        ),
        in_specs=[kept] * 2,
        out_specs=(kept, kept),
        scratch_shapes=[dma((2,))],
        compiler_params=pltpu.CompilerParams(vmem_limit_bytes=1 << 20),
    )(*results)


def solution(mesh):
    spec4, spec3 = P(None, None, "tile", "col"), P(None, "tile", "col")
    return jax.shard_map(
        functools.partial(on_device, mesh.shape["col"], mesh.shape["tile"]),
        mesh=mesh,
        in_specs=(spec4, spec3, spec4, spec4, spec4),
        out_specs=(spec4, P()),
        check_vma=False,
    )
```

```python
import functools

import jax
import jax.numpy as jnp
from jax import lax
from jax.experimental import pallas as pl
from jax.experimental.pallas import tpu as pltpu
from jax.sharding import PartitionSpec as P

RIM = 2
STEPS = 3
WIDE = 3 * STEPS
BESIDE = [(0, 1), (0, -1), (1, 0), (-1, 0)]
LANES = 128
CODES = 18
MESH = pl.DeviceIdType.MESH
BONDS = ((0, 0), (-1, 0), (0, -1))
HOP, CODE, SITE, BOND2 = 4, 5, 6, 7


def relay_rounds(n_col, n_tile):
    rounds = [BESIDE]
    col, tile = 1, 1
    while col < n_col // 2 or tile < n_tile // 2:
        cols = (0, -col, col) if col < n_col // 2 else (0,)
        tiles = (0, -tile, tile) if tile < n_tile // 2 else (0,)
        rounds.append([(c, t) for c in cols for t in tiles if (c, t) != (0, 0)])
        col, tile = 2 * col, 2 * tile
    return rounds


def kernel(
    n_col, n_tile, orbitals,
    v_hbm, onsite_hbm, intra_hbm, index_hbm, hop_hbm,
    out_ref, mom_ref,
    v_ref, onsite_ref, intra_ref, index_ref, hop_ref, load_sem,
    area, term1, term2, term3, moved0, moved1, moved2, weights, weights_t, bond_t,
    packs, halo, tile_packs, tile_halo, strips, strip_site, strip_weights, sums, part, all_parts,
    row_send, row_recv, pack_send, pack_recv, tile_send, tile_recv, part_send, part_recv, relay,
):
    rows = v_ref.shape[2]
    cols = v_ref.shape[3]
    blocks = cols // LANES
    my_col = lax.axis_index("col")
    my_tile = lax.axis_index("tile")
    lane = lax.broadcasted_iota(jnp.int32, (8, LANES), 1)
    sub = lax.broadcasted_iota(jnp.int32, (8, LANES), 0)

    def col_at(step):
        return lax.rem(my_col + step + n_col, n_col)

    def tile_at(step):
        return lax.rem(my_tile + step + n_tile, n_tile)

    barrier = pltpu.get_barrier_semaphore()
    devices = n_col * n_tile
    me = my_col * n_tile + my_tile

    def device(step):
        at = lax.rem(me + step, devices)
        return (lax.div(at, n_tile), lax.rem(at, n_tile))

    def signal(semaphore, offsets):
        for c, t in offsets:
            pl.semaphore_signal(semaphore, inc=1, device_id=(col_at(c), tile_at(t)), device_id_type=MESH)

    signal(barrier, BESIDE)

    rounds = relay_rounds(n_col, n_tile)
    done = [0]

    def tell():
        if done[0] < len(rounds):
            signal(relay.at[done[0]], rounds[done[0]])

    def relay_on():
        if done[0] < len(rounds):
            pl.semaphore_wait(relay.at[done[0]], len(rounds[done[0]]))
            done[0] += 1
            tell()

    loads = [
        pltpu.make_async_copy(src, dst, load_sem.at[n])
        for n, (src, dst) in enumerate(
            (
                (v_hbm, v_ref),
                (hop_hbm, hop_ref),
                (index_hbm, index_ref),
                (onsite_hbm, onsite_ref),
                (intra_hbm, intra_ref),
            )
        )
    ]
    for load in loads:
        load.start()

    for load in loads:
        load.wait()
    own = slice(RIM, RIM + rows)
    for o in range(4):
        area[o, own, :, 0:cols] = jnp.swapaxes(v_ref[:, o], 0, 1)
    area[HOP, own, :, 0:cols] = jnp.swapaxes(hop_ref[...], 0, 1)
    area[CODE, own, :, 0:cols] = jnp.swapaxes(index_ref[...].astype(jnp.float32), 0, 1)
    area[SITE, own, :, 0:cols] = jnp.swapaxes(
        jnp.concatenate([onsite_ref[...], intra_ref[0:4]], axis=0), 0, 1
    )
    area[BOND2, own, :, 0:cols] = jnp.swapaxes(
        jnp.concatenate(
            [intra_ref[4:6], pltpu.roll(intra_ref[2:4], rows - 1, 1), jnp.zeros((4, rows, cols), jnp.float32)], axis=0
        ),
        0,
        1,
    )

    first, last, half = lane == 0, lane == LANES - 1, lane < LANES // 2
    terms = (term1, term2, term3)
    moved = (moved0, moved1, moved2)

    def block(b):
        return slice(b * LANES, (b + 1) * LANES)

    zero = jnp.zeros((8, LANES), jnp.float32)

    def shift(x, by):
        by = by % LANES
        return pltpu.roll(x, by, 1) if by else x

    def over(x):
        return functools.reduce(jnp.add, [jnp.where(x >= WIDE * n, 1, 0) for n in range(1, LANES // WIDE + 1)])

    turned = jnp.where(lane >= LANES - STEPS, lane - (LANES - STEPS), lane + STEPS)
    strip_row = [over(lane), over(turned)]
    within = lane - WIDE * strip_row[0]
    strip_col = [within, turned - WIDE * strip_row[1]]
    lefts, mids = within < STEPS, (within >= STEPS) & (within < 2 * STEPS)
    own_cols = [strip_col[0] >= STEPS, strip_col[1] < 2 * STEPS]
    above = [strip_row[n] < STEPS for n in range(2)]
    below = [strip_row[n] >= STEPS + rows for n in range(2)]

    def build_strips():
        for g in range(8):
            kept = [zero, zero]
            for i in range(rows):
                edges = jnp.where(half, area[g, RIM + i, :, 0:LANES], area[g, RIM + i, :, cols - LANES : cols])
                edges = shift(edges, WIDE * (i + STEPS) + STEPS)
                for n in range(2):
                    kept[n] = jnp.where((strip_row[n] == i + STEPS) & own_cols[n], edges, kept[n])
            for n in range(2):
                strips[n, g] = kept[n]
        for n in range(3):
            for side in range(2):
                x = strips[side, 3 * n]
                y = shift(strips[side, 3 * n + 1], STEPS)
                z = strips[side, 3 * n + 2] if n < 2 else zero
                z = shift(z, -STEPS if side == 0 else 2 * STEPS)
                if side == 0:
                    packs[side, n] = jnp.where(lefts, z, jnp.where(mids, x, y))
                else:
                    packs[side, n] = jnp.where(lefts, x, jnp.where(mids, y, z))

    def build_tile_packs():
        for way in range(2):
            start = WIDE * (rows if way == 0 else STEPS)
            for n in range(4):
                x = zero
                for j in range(4):
                    side, g = (4 * n + j) // 8, (4 * n + j) % 8
                    y = shift(strips[side, g], 32 * j - start + STEPS * side)
                    x = jnp.where(lane // 32 == j, y, x)
                tile_packs[way, n] = x

    code_of = [(3 * sub + g).astype(jnp.float32) for g in range(3)]

    def weigh_of(codes, hops, s):
        total = [None] * 3
        for k in range(4):
            f = 2 * k + s
            code = jnp.broadcast_to(codes(f), (8, LANES))
            hop = jnp.broadcast_to(hops(f), (8, LANES))
            for g in range(3):
                x = jnp.where(code == code_of[g], hop, 0.0)
                total[g] = x if k == 0 else total[g] + x
        return total

    def weigh(r, s, b):
        at = block(b)
        total = weigh_of(lambda f: area[CODE, r, f : f + 1, at], lambda f: area[HOP, r, f : f + 1, at], s)
        for g in range(3):
            weights[r, s, 8 * g : 8 * g + 8, at] = total[g]
        return total

    def back(x):
        return pltpu.roll(x, 1, 1)

    def ahead(x):
        return pltpu.roll(x, LANES - 1, 1)

    def loop(low, high, body):
        def step(i, carry):
            body(i)
            return carry

        lax.fori_loop(low, high, step, 0)

    low, high = RIM, RIM + rows
    def put(ref, at, b, x):
        ref[(*at, slice(None), block(b))] = x

    def own_turns(xs, way, store):
        if way < 0:
            ys = [back(x) for x in xs]
            for b in range(blocks):
                store(b, ys[b] if b == 0 else jnp.where(first, ys[b - 1], ys[b]))
        else:
            ys = [ahead(x) for x in xs]
            for b in range(blocks):
                store(b, ys[b] if b == blocks - 1 else jnp.where(last, ys[b + 1], ys[b]))

    def field(g, r):
        return [area[g, r, :, block(b)] for b in range(blocks)]

    def moved_at(ref, at):
        return lambda b, x: put(ref, at, b, x)

    def weights_at(r, s, g):
        def store(b, x):
            weights_t[r, s, 8 * g : 8 * g + 8, block(b)] = x
        return store

    def bond_at(r):
        def store(b, x):
            bond_t[r, :, block(b)] = x
        return store

    def prepare(r, bonds=True):
        for s in range(2):
            totals = [weigh(r, s, b) for b in range(blocks)]
            own_turns([t[0] for t in totals], 1, weights_at(r, s, 0))
            own_turns([t[2] for t in totals], -1, weights_at(r, s, 1))
        for o in range(4):
            xs = field(o, r)
            own_turns(xs, -1, moved_at(moved0, (0, o, r)))
            own_turns(xs, 1, moved_at(moved0, (1, o, r)))
        if bonds:
            own_turns(field(BOND2, r), 1, bond_at(r))

    for n in range(7):
        sums[n] = zero

    pl.semaphore_wait(barrier, len(BESIDE))
    tell()

    near = lax.rem(my_tile, 2)
    far = 1 - near

    def edge(way):
        return jnp.where(way == 0, low, high - 1), 2 * way - 1

    def rim(layer, way):
        deep = 1 if layer == 2 else layer
        src = jnp.where(way == 0, high - 1 - deep, low + deep)
        row, out = edge(way)
        dst = row + out * (min(layer, 1) + 1)
        if layer == 2:
            src_ref = term1.at[:, pl.ds(src, 1), :, 0:cols]
            dst_ref = term1.at[:, pl.ds(dst, 1), :, 0:cols]
        else:
            groups = 8 if layer == 0 else 6
            src_ref = area.at[0:groups, pl.ds(src, 1), :, 0:cols]
            dst_ref = area.at[0:groups, pl.ds(dst, 1), :, 0:cols]
        return pltpu.make_async_remote_copy(
            src_ref=src_ref,
            dst_ref=dst_ref,
            send_sem=row_send.at[layer, way],
            recv_sem=row_recv.at[layer, way],
            device_id=(my_col, tile_at(1 - 2 * way)),
            device_id_type=MESH,
        )

    for layer, away in ((0, 1), (0, 0), (1, 1), (1, 0)):
        rim(layer, far if away else near).start()

    pack_copies = {}

    def send_packs(tiles):
        for side, step in ((0, -1), (1, 1)):
            for dt in tiles:
                slot = side * 3 + 1 - dt
                copy = pltpu.make_async_remote_copy(
                    src_ref=packs.at[side],
                    dst_ref=halo.at[slot],
                    send_sem=pack_send.at[slot],
                    recv_sem=pack_recv.at[slot],
                    device_id=(col_at(step), tile_at(dt)),
                    device_id_type=MESH,
                )
                copy.start()
                pack_copies[side, dt] = copy

    build_strips()
    send_packs((0,))
    build_tile_packs()
    tile_copies = []
    for way in range(2):
        copy = pltpu.make_async_remote_copy(
            src_ref=tile_packs.at[way],
            dst_ref=tile_halo.at[way],
            send_sem=tile_send.at[way],
            recv_sem=tile_recv.at[way],
            device_id=(my_col, tile_at(1 - 2 * way)),
            device_id_type=MESH,
        )
        copy.start()
        tile_copies.append(copy)

    loop(low, high, prepare)
    relay_on()
    send_packs((-1, 1))

    def term(k, o, r, at):
        return area[o, r, :, at] if k == 0 else terms[k - 1][o, r, :, at]

    def hamiltonian(k, r, at):
        def v(o, row_off, col_off):
            if col_off == 0:
                return term(k, o, r + row_off, at)
            return moved[k][(col_off + 1) // 2, o, r + row_off, :, at]

        def spread(x):
            return jnp.broadcast_to(x, (8, LANES))

        def site(f, row):
            return spread(area[SITE, row, f : f + 1, at])

        outs = []
        for l in range(2):
            a, b = 2 * l, 2 * l + 1
            f0, f1 = site(4 + l, r), site(6 + l, r)
            f2 = spread(area[BOND2, r, l : l + 1, at])
            outs.append(
                site(a, r) * v(a, 0, 0) + f0 * v(b, 0, 0) + f1 * v(b, -1, 0) + f2 * v(b, 0, -1)
            )
            outs.append(
                site(b, r) * v(b, 0, 0)
                + f0 * v(a, 0, 0)
                + site(6 + l, r + 1) * v(a, 1, 0)
                + spread(bond_t[r, l : l + 1, at]) * v(a, 0, 1)
            )
        for s in range(2):
            for c in range(CODES):
                t, e, f = c // 9, c % 9 // 3 - 1, c % 3 - 1
                n = 8 * (f + 1) + 3 * t + e + 1
                outs[s] = outs[s] + spread(weights[r, s, n : n + 1, at]) * v(2 + t, e, f)
                if f == 0:
                    other = weights[r - e, s, n : n + 1, at]
                else:
                    n = 4 * (f + 1) + 3 * t + e + 1
                    other = weights_t[r - e, s, n : n + 1, at]
                outs[2 + t] = outs[2 + t] + spread(other) * v(s, -e, -f)
        return outs

    def advance(k, r):
        inside = jnp.where((r >= RIM) & (r < RIM + rows), 1.0, 0.0).astype(jnp.float32)
        cross, square, first_sum = zero, zero, zero
        turns = [{} for _ in range(4)]

        def store_turn(o, way, b):
            near = turns[o][b][(way + 1) // 2]
            if 0 <= b + way < blocks:
                near = jnp.where(first if way < 0 else last, turns[o][b + way][(way + 1) // 2], near)
            moved[k + 1][(way + 1) // 2, o, r, :, block(b)] = near

        for b in range(blocks):
            at = block(b)
            outs = hamiltonian(k, r, at)
            crosses, squares = zero, zero
            for o in range(4):
                old = term(k, o, r, at)
                new = outs[o] if k == 0 else 2.0 * outs[o] - term(k - 1, o, r, at)
                terms[k][o, r, :, at] = new
                crosses = crosses + new * old
                squares = squares + new * new
                if k == 0:
                    first_sum = first_sum + old * old
                if k < 2:
                    turns[o][b] = (back(new), ahead(new))
                    store_turn(o, -1, b)
                    if b > 0:
                        store_turn(o, 1, b - 1)
            if b == 0:
                crosses, squares = (jnp.where(lane > k, x, 0.0) for x in (crosses, squares))
            if b == blocks - 1:
                crosses, squares = (jnp.where(lane < LANES - 1 - k, x, 0.0) for x in (crosses, squares))
            cross, square = cross + crosses, square + squares
        if k < 2:
            for o in range(4):
                store_turn(o, 1, blocks - 1)
        if k == 0:
            sums[0] += inside * first_sum
        sums[2 * k + 1] += inside * cross
        sums[2 * k + 2] += inside * square

    def strip_terms(n):
        sides = [
            [halo[3 * (1 - n) + m, i] for i in range(3)] for m in range(3)
        ]
        side = [
            jnp.where(
                above[0], shift(sides[0][i], -WIDE * rows), jnp.where(below[0], shift(sides[2][i], WIDE * rows), sides[1][i])
            )
            for i in range(3)
        ]
        turns = (0, -STEPS, -2 * STEPS) if n == 0 else (0, -STEPS, STEPS)
        fields = []
        for g in range(8):
            m, j = divmod(8 * n + g, 4)
            top = shift(tile_halo[0, m], -32 * j - STEPS * n)
            bottom = shift(tile_halo[1, m], WIDE * (STEPS + rows) - 32 * j - STEPS * n)
            x = jnp.where(above[n], top, jnp.where(below[n], bottom, strips[n, g]))
            fields.append(jnp.where(mids if n else lefts, shift(side[g // 3], turns[g % 3]), x))
        strip_site[n, 0], strip_site[n, 1] = fields[SITE], fields[BOND2]
        strips[n, HOP], strips[n, CODE] = fields[HOP], fields[CODE]
        for s in range(2):
            totals = weigh_of(lambda f: strips[n, CODE, f : f + 1], lambda f: strips[n, HOP, f : f + 1], s)
            for g in range(3):
                strip_weights[n, s, 8 * g : 8 * g + 8] = totals[g]

        def spread(x):
            return jnp.broadcast_to(x, (8, LANES))

        def at(x, e, f):
            return shift(x, -(WIDE * e + f))

        def apply(v):
            outs = [None] * 4
            for l in range(2):
                a, b = 2 * l, 2 * l + 1
                sa, sb, f0, f1 = (spread(strip_site[n, 0, i : i + 1]) for i in (a, b, 4 + l, 6 + l))
                f2 = spread(strip_site[n, 1, l : l + 1])
                outs[a] = sa * v[a] + f0 * v[b] + f1 * at(v[b], -1, 0) + f2 * at(v[b], 0, -1)
                outs[b] = sb * v[b] + f0 * v[a] + at(f1 * v[a], 1, 0) + at(f2 * v[a], 0, 1)
            for c in range(CODES):
                t, e, f = c // 9, c % 9 // 3 - 1, c % 3 - 1
                i = 8 * (f + 1) + 3 * t + e + 1
                w = [spread(strip_weights[n, s, i : i + 1]) for s in range(2)]
                far = at(v[2 + t], e, f)
                for s in range(2):
                    outs[s] = outs[s] + w[s] * far
                outs[2 + t] = outs[2 + t] + at(w[0] * v[0] + w[1] * v[1], -e, -f)
            return outs

        older, old = None, fields[0:4]
        for k in range(3):
            outs = apply(old)
            new = outs if k == 0 else [2.0 * outs[o] - older[o] for o in range(4)]
            col = strip_col[n] - (STEPS if n == 0 else 0)
            wanted = (col >= 0) & (col <= k) if n == 0 else (col >= 5 - k) & (col <= 5)
            wanted = wanted & ~above[n] & ~below[n]
            cross = functools.reduce(jnp.add, [new[o] * old[o] for o in range(4)])
            square = functools.reduce(jnp.add, [new[o] * new[o] for o in range(4)])
            sums[2 * k + 1] += jnp.where(wanted, cross, 0.0)
            sums[2 * k + 2] += jnp.where(wanted, square, 0.0)
            older, old = old, new
        for o in range(4):
            strips[n, o] = old[o]

    loop(0, 2, lambda i: advance(0, low + 1 + i * (rows - 3)))
    rim(2, far).start()
    rim(2, near).start()
    loop(low + 2, high - 2, functools.partial(advance, 0))
    relay_on()
    for k in (1, 2):
        loop(low + 1 + k, high - 1 - k, functools.partial(advance, k))

    def rims(i):
        way = jnp.where(i == 0, far, near)
        row, out = edge(way)
        for layer in range(3):
            rim(layer, way).wait_recv()
            r = row + out * (min(layer, 1) + 1)
            if layer < 2:
                prepare(r, layer == 0)
                if layer == 0:
                    area[SITE, r + out, 6:8, 0:cols] = area[BOND2, r, 2:4, 0:cols]
            else:
                for o in range(4):
                    xs = [term1[o, r, :, block(b)] for b in range(blocks)]
                    own_turns(xs, -1, moved_at(moved1, (0, o, r)))
                    own_turns(xs, 1, moved_at(moved1, (1, o, r)))
            for k in range(1 if layer == 2 else 0, 3):
                advance(k, row + out * (layer - k))

        @pl.when(i == 0)
        def _():
            for copy in pack_copies.values():
                copy.wait_recv()
            for copy in tile_copies:
                copy.wait_recv()
            for n in range(2):
                strip_terms(n)

    loop(0, 2, rims)

    row = jnp.zeros((8, LANES), jnp.float32)
    for n in range(7):
        total = jnp.sum(sums[n], axis=1, keepdims=True)
        row = jnp.where(lane == sub + 8 * n, jnp.broadcast_to(total, (8, LANES)), row)
    part[...] = jnp.sum(row, axis=0, keepdims=True)
    all_parts[me] = part[...]

    def other(step):
        at = jnp.where(step > me, step, step - 1)
        return (lax.div(at, n_tile), lax.rem(at, n_tile))

    def part_copy(step):
        return pltpu.make_async_remote_copy(
            src_ref=part,
            dst_ref=all_parts.at[me],
            send_sem=part_send,
            recv_sem=part_recv,
            device_id=other(step),
            device_id_type=MESH,
        )

    while done[0] < len(rounds):
        relay_on()
    loop(1, devices, lambda i: part_copy(i).start())
    for o in range(4):
        both = jnp.where(lefts, strips[1, o], strips[0, o])
        for i in range(rows):
            x = shift(both, -(WIDE * (i + STEPS) + STEPS))
            term3[o, low + i, :, 0:LANES] = jnp.where(lane < STEPS, x, term3[o, low + i, :, 0:LANES])
            edge_at = slice(cols - LANES, cols)
            term3[o, low + i, :, edge_at] = jnp.where(lane >= LANES - STEPS, x, term3[o, low + i, :, edge_at])
    for o in range(4):
        out_ref[:, o] = jnp.swapaxes(term3[o, own, :, 0:cols], 0, 1)

    for copy in (*pack_copies.values(), *tile_copies):
        copy.wait_send()
    for layer in range(3):
        for way in range(2):
            rim(layer, way).wait_send()
    arrived = pltpu.make_async_remote_copy(
        src_ref=all_parts.at[1:devices],
        dst_ref=all_parts.at[1:devices],
        send_sem=part_send,
        recv_sem=part_recv,
        device_id=device(1),
        device_id_type=MESH,
    )
    arrived.wait_recv()
    arrived.wait_send()
    pieces = [all_parts[n] for n in range(devices)]
    while len(pieces) > 1:
        half_way = (len(pieces) + 1) // 2
        pieces = [
            pieces[n] + pieces[n + half_way] if n + half_way < len(pieces) else pieces[n]
            for n in range(half_way)
        ]
    total = pieces[0]
    total = jnp.broadcast_to(total / orbitals, (8, LANES))
    scaled = [pltpu.roll(total, (LANES - 8 * n) % LANES, 1)[0:1, 0:8] for n in range(7)]
    mom_ref[0:1, :] = scaled[0]
    mom_ref[1:2, :] = scaled[1]
    for n in range(2, 7):
        mom_ref[n : n + 1, :] = 2.0 * scaled[n] - scaled[n % 2]


def emit(last_ref, rows_ref, out_ref, mom_ref, sem):
    copies = [
        pltpu.make_async_copy(last_ref, out_ref, sem.at[0]),
        pltpu.make_async_copy(rows_ref, mom_ref, sem.at[1]),
    ]
    for copy in copies:
        copy.start()
    for copy in copies:
        copy.wait()


def on_device(n_col, n_tile, vectors, onsite, intra_hop, inter_index, inter_hop):
    count, _, rows, cols = vectors.shape
    slots = inter_index.shape[0]
    assert n_col > 2 and n_tile > 2
    assert count == 8 and slots == 4 and rows == 8 and cols % LANES == 0
    tall = rows + 2 * RIM
    ring = cols + LANES
    f32 = jnp.float32
    vmem = pl.BlockSpec(memory_space=pltpu.VMEM)
    dma = pltpu.SemaphoreType.DMA
    results = pl.pallas_call(
        functools.partial(kernel, n_col, n_tile, 4 * rows * cols * n_col * n_tile),
        out_shape=(
            jax.ShapeDtypeStruct(vectors.shape, f32),
            jax.ShapeDtypeStruct((7, count), f32),
        ),
        in_specs=[pl.BlockSpec(memory_space=pltpu.HBM)] * 5,
        out_specs=(vmem, vmem),
        scratch_shapes=[
            pltpu.VMEM(vectors.shape, f32),
            pltpu.VMEM(onsite.shape, f32),
            pltpu.VMEM((6, rows, cols), f32),
            pltpu.VMEM((2 * slots, rows, cols), jnp.int32),
            pltpu.VMEM((2 * slots, rows, cols), f32),
            dma((5,)),
            pltpu.VMEM((8, tall, 8, ring), f32),
            *[pltpu.VMEM((4, tall, 8, ring), f32)] * 3,
            *[pltpu.VMEM((2, 4, tall, 8, ring), f32)] * 3,
            pltpu.VMEM((tall, 2, 24, ring), f32),
            pltpu.VMEM((tall, 2, 16, ring), f32),
            pltpu.VMEM((tall, 8, ring), f32),
            pltpu.VMEM((2, 3, 8, LANES), f32),
            pltpu.VMEM((6, 3, 8, LANES), f32),
            pltpu.VMEM((2, 4, 8, LANES), f32),
            pltpu.VMEM((2, 4, 8, LANES), f32),
            pltpu.VMEM((2, 8, 8, LANES), f32),
            pltpu.VMEM((2, 2, 8, LANES), f32),
            pltpu.VMEM((2, 2, 24, LANES), f32),
            pltpu.VMEM((7, 8, LANES), f32),
            pltpu.VMEM((1, LANES), f32),
            pltpu.VMEM((n_col * n_tile, 1, LANES), f32),
            dma((3, 2)), dma((3, 2)), dma((6,)), dma((6,)), dma((2,)), dma((2,)), dma, dma,
            pltpu.SemaphoreType.REGULAR((len(relay_rounds(n_col, n_tile)),)),
        ],
        compiler_params=pltpu.CompilerParams(
            collective_id=0, has_side_effects=True, vmem_limit_bytes=32 << 20
        ),
    )(
        *(
            pltpu.with_memory_space_constraint(x, pltpu.HBM)
            for x in (
                vectors,
                onsite,
                intra_hop.reshape(6, rows, cols),
                inter_index.reshape(2 * slots, rows, cols),
                inter_hop.reshape(2 * slots, rows, cols),
            )
        )
    )
    kept = pl.BlockSpec(memory_space=pl.ANY)
    return pl.pallas_call(
        emit,
        out_shape=(
            jax.ShapeDtypeStruct(vectors.shape, f32),
            jax.ShapeDtypeStruct((7, count), f32),
        ),
        in_specs=[kept] * 2,
        out_specs=(kept, kept),
        scratch_shapes=[dma((2,))],
        compiler_params=pltpu.CompilerParams(vmem_limit_bytes=1 << 20),
    )(*results)


def solution(mesh):
    spec4, spec3 = P(None, None, "tile", "col"), P(None, "tile", "col")
    return jax.shard_map(
        functools.partial(on_device, mesh.shape["col"], mesh.shape["tile"]),
        mesh=mesh,
        in_specs=(spec4, spec3, spec4, spec4, spec4),
        out_specs=(spec4, P()),
        check_vma=False,
    )
```

```python
import functools

import jax
import jax.numpy as jnp
from jax import lax
from jax.experimental import pallas as pl
from jax.experimental.pallas import tpu as pltpu
from jax.sharding import PartitionSpec as P

RIM = 2
STEPS = 3
WIDE = 3 * STEPS
BESIDE = [(0, 1), (0, -1), (1, 0), (-1, 0)]
LANES = 128
CODES = 18
MESH = pl.DeviceIdType.MESH
BONDS = ((0, 0), (-1, 0), (0, -1))
HOP, CODE, SITE, BOND2 = 4, 5, 6, 7


def relay_rounds(n_col, n_tile):
    rounds = [BESIDE]
    col, tile = 1, 1
    while col < n_col // 2 or tile < n_tile // 2:
        cols = (0, -col, col) if col < n_col // 2 else (0,)
        tiles = (0, -tile, tile) if tile < n_tile // 2 else (0,)
        rounds.append([(c, t) for c in cols for t in tiles if (c, t) != (0, 0)])
        col, tile = 2 * col, 2 * tile
    return rounds


def kernel(
    n_col, n_tile, orbitals,
    v_hbm, onsite_hbm, intra_hbm, index_hbm, hop_hbm,
    out_ref, mom_ref,
    v_ref, onsite_ref, intra_ref, index_ref, hop_ref, load_sem,
    area, term1, term2, term3, moved0, moved1, moved2, weights, weights_t, bond_t,
    packs, halo, tile_packs, tile_halo, strips, strip_site, strip_weights, sums, part, all_parts,
    row_send, row_recv, pack_send, pack_recv, tile_send, tile_recv, part_send, part_recv, relay,
):
    rows = v_ref.shape[2]
    cols = v_ref.shape[3]
    blocks = cols // LANES
    my_col = lax.axis_index("col")
    my_tile = lax.axis_index("tile")
    lane = lax.broadcasted_iota(jnp.int32, (8, LANES), 1)
    sub = lax.broadcasted_iota(jnp.int32, (8, LANES), 0)

    def col_at(step):
        return lax.rem(my_col + step + n_col, n_col)

    def tile_at(step):
        return lax.rem(my_tile + step + n_tile, n_tile)

    barrier = pltpu.get_barrier_semaphore()
    devices = n_col * n_tile
    me = my_col * n_tile + my_tile

    def device(step):
        at = lax.rem(me + step, devices)
        return (lax.div(at, n_tile), lax.rem(at, n_tile))

    def signal(semaphore, offsets):
        for c, t in offsets:
            pl.semaphore_signal(semaphore, inc=1, device_id=(col_at(c), tile_at(t)), device_id_type=MESH)

    signal(barrier, BESIDE)

    rounds = relay_rounds(n_col, n_tile)
    done = [0]

    def tell():
        if done[0] < len(rounds):
            signal(relay.at[done[0]], rounds[done[0]])

    def relay_on():
        if done[0] < len(rounds):
            pl.semaphore_wait(relay.at[done[0]], len(rounds[done[0]]))
            done[0] += 1
            tell()

    loads = [
        pltpu.make_async_copy(src, dst, load_sem.at[n])
        for n, (src, dst) in enumerate(
            (
                (v_hbm, v_ref),
                (hop_hbm, hop_ref),
                (index_hbm, index_ref),
                (onsite_hbm, onsite_ref),
                (intra_hbm, intra_ref),
            )
        )
    ]
    for load in loads:
        load.start()

    for load in loads:
        load.wait()
    own = slice(RIM, RIM + rows)
    for o in range(4):
        area[o, own, :, 0:cols] = jnp.swapaxes(v_ref[:, o], 0, 1)
    area[HOP, own, :, 0:cols] = jnp.swapaxes(hop_ref[...], 0, 1)
    area[CODE, own, :, 0:cols] = jnp.swapaxes(index_ref[...].astype(jnp.float32), 0, 1)
    area[SITE, own, :, 0:cols] = jnp.swapaxes(
        jnp.concatenate([onsite_ref[...], intra_ref[0:4]], axis=0), 0, 1
    )
    area[BOND2, own, :, 0:cols] = jnp.swapaxes(
        jnp.concatenate(
            [intra_ref[4:6], pltpu.roll(intra_ref[2:4], rows - 1, 1), jnp.zeros((4, rows, cols), jnp.float32)], axis=0
        ),
        0,
        1,
    )

    first, last, half = lane == 0, lane == LANES - 1, lane < LANES // 2
    terms = (term1, term2, term3)
    moved = (moved0, moved1, moved2)

    def block(b):
        return slice(b * LANES, (b + 1) * LANES)

    zero = jnp.zeros((8, LANES), jnp.float32)

    def shift(x, by):
        by = by % LANES
        return pltpu.roll(x, by, 1) if by else x

    def over(x):
        return functools.reduce(jnp.add, [jnp.where(x >= WIDE * n, 1, 0) for n in range(1, LANES // WIDE + 1)])

    turned = jnp.where(lane >= LANES - STEPS, lane - (LANES - STEPS), lane + STEPS)
    strip_row = [over(lane), over(turned)]
    within = lane - WIDE * strip_row[0]
    strip_col = [within, turned - WIDE * strip_row[1]]
    lefts, mids = within < STEPS, (within >= STEPS) & (within < 2 * STEPS)
    own_cols = [strip_col[0] >= STEPS, strip_col[1] < 2 * STEPS]
    above = [strip_row[n] < STEPS for n in range(2)]
    below = [strip_row[n] >= STEPS + rows for n in range(2)]

    def build_strips():
        for g in range(8):
            kept = [zero, zero]
            for i in range(rows):
                edges = jnp.where(half, area[g, RIM + i, :, 0:LANES], area[g, RIM + i, :, cols - LANES : cols])
                edges = shift(edges, WIDE * (i + STEPS) + STEPS)
                for n in range(2):
                    kept[n] = jnp.where((strip_row[n] == i + STEPS) & own_cols[n], edges, kept[n])
            for n in range(2):
                strips[n, g] = kept[n]
        for n in range(3):
            for side in range(2):
                x = strips[side, 3 * n]
                y = shift(strips[side, 3 * n + 1], STEPS)
                z = strips[side, 3 * n + 2] if n < 2 else zero
                z = shift(z, -STEPS if side == 0 else 2 * STEPS)
                if side == 0:
                    packs[side, n] = jnp.where(lefts, z, jnp.where(mids, x, y))
                else:
                    packs[side, n] = jnp.where(lefts, x, jnp.where(mids, y, z))

    def build_tile_packs():
        for way in range(2):
            start = WIDE * (rows if way == 0 else STEPS)
            for n in range(4):
                x = zero
                for j in range(4):
                    side, g = (4 * n + j) // 8, (4 * n + j) % 8
                    y = shift(strips[side, g], 32 * j - start + STEPS * side)
                    x = jnp.where(lane // 32 == j, y, x)
                tile_packs[way, n] = x

    code_of = [(3 * sub + g).astype(jnp.float32) for g in range(3)]

    def weigh_of(codes, hops, s):
        total = [None] * 3
        for k in range(4):
            f = 2 * k + s
            code = jnp.broadcast_to(codes(f), (8, LANES))
            hop = jnp.broadcast_to(hops(f), (8, LANES))
            for g in range(3):
                x = jnp.where(code == code_of[g], hop, 0.0)
                total[g] = x if k == 0 else total[g] + x
        return total

    def weigh(r, s, b):
        at = block(b)
        total = weigh_of(lambda f: area[CODE, r, f : f + 1, at], lambda f: area[HOP, r, f : f + 1, at], s)
        for g in range(3):
            weights[r, s, 8 * g : 8 * g + 8, at] = total[g]
        return total

    def back(x):
        return pltpu.roll(x, 1, 1)

    def ahead(x):
        return pltpu.roll(x, LANES - 1, 1)

    def loop(low, high, body):
        def step(i, carry):
            body(i)
            return carry

        lax.fori_loop(low, high, step, 0)

    low, high = RIM, RIM + rows
    def put(ref, at, b, x):
        ref[(*at, slice(None), block(b))] = x

    def own_turns(xs, way, store):
        if way < 0:
            ys = [back(x) for x in xs]
            for b in range(blocks):
                store(b, ys[b] if b == 0 else jnp.where(first, ys[b - 1], ys[b]))
        else:
            ys = [ahead(x) for x in xs]
            for b in range(blocks):
                store(b, ys[b] if b == blocks - 1 else jnp.where(last, ys[b + 1], ys[b]))

    def field(g, r):
        return [area[g, r, :, block(b)] for b in range(blocks)]

    def moved_at(ref, at):
        return lambda b, x: put(ref, at, b, x)

    def weights_at(r, s, g):
        def store(b, x):
            weights_t[r, s, 8 * g : 8 * g + 8, block(b)] = x
        return store

    def bond_at(r):
        def store(b, x):
            bond_t[r, :, block(b)] = x
        return store

    def prepare(r, bonds=True):
        for s in range(2):
            totals = [weigh(r, s, b) for b in range(blocks)]
            own_turns([t[0] for t in totals], 1, weights_at(r, s, 0))
            own_turns([t[2] for t in totals], -1, weights_at(r, s, 1))
        for o in range(4):
            xs = field(o, r)
            own_turns(xs, -1, moved_at(moved0, (0, o, r)))
            own_turns(xs, 1, moved_at(moved0, (1, o, r)))
        if bonds:
            own_turns(field(BOND2, r), 1, bond_at(r))

    for n in range(7):
        sums[n] = zero

    pl.semaphore_wait(barrier, len(BESIDE))
    tell()

    near = lax.rem(my_tile, 2)
    far = 1 - near

    def edge(way):
        return jnp.where(way == 0, low, high - 1), 2 * way - 1

    def rim(layer, way):
        deep = 1 if layer == 2 else layer
        src = jnp.where(way == 0, high - 1 - deep, low + deep)
        row, out = edge(way)
        dst = row + out * (min(layer, 1) + 1)
        if layer == 2:
            src_ref = term1.at[:, pl.ds(src, 1), :, 0:cols]
            dst_ref = term1.at[:, pl.ds(dst, 1), :, 0:cols]
        else:
            groups = 8 if layer == 0 else 6
            src_ref = area.at[0:groups, pl.ds(src, 1), :, 0:cols]
            dst_ref = area.at[0:groups, pl.ds(dst, 1), :, 0:cols]
        return pltpu.make_async_remote_copy(
            src_ref=src_ref,
            dst_ref=dst_ref,
            send_sem=row_send.at[layer, way],
            recv_sem=row_recv.at[layer, way],
            device_id=(my_col, tile_at(1 - 2 * way)),
            device_id_type=MESH,
        )

    for layer, away in ((0, 1), (0, 0), (1, 1), (1, 0)):
        rim(layer, far if away else near).start()

    pack_copies = {}

    def send_packs(tiles):
        for side, step in ((0, -1), (1, 1)):
            for dt in tiles:
                slot = side * 3 + 1 - dt
                copy = pltpu.make_async_remote_copy(
                    src_ref=packs.at[side],
                    dst_ref=halo.at[slot],
                    send_sem=pack_send.at[slot],
                    recv_sem=pack_recv.at[slot],
                    device_id=(col_at(step), tile_at(dt)),
                    device_id_type=MESH,
                )
                copy.start()
                pack_copies[side, dt] = copy

    build_strips()
    send_packs((0,))
    build_tile_packs()
    tile_copies = []
    for way in range(2):
        copy = pltpu.make_async_remote_copy(
            src_ref=tile_packs.at[way],
            dst_ref=tile_halo.at[way],
            send_sem=tile_send.at[way],
            recv_sem=tile_recv.at[way],
            device_id=(my_col, tile_at(1 - 2 * way)),
            device_id_type=MESH,
        )
        copy.start()
        tile_copies.append(copy)

    loop(low, high, prepare)
    relay_on()
    send_packs((-1, 1))

    def term(k, o, r, at):
        return area[o, r, :, at] if k == 0 else terms[k - 1][o, r, :, at]

    def hamiltonian(k, r, at):
        def v(o, row_off, col_off):
            if col_off == 0:
                return term(k, o, r + row_off, at)
            return moved[k][(col_off + 1) // 2, o, r + row_off, :, at]

        def spread(x):
            return jnp.broadcast_to(x, (8, LANES))

        def site(f, row):
            return spread(area[SITE, row, f : f + 1, at])

        outs = []
        for l in range(2):
            a, b = 2 * l, 2 * l + 1
            f0, f1 = site(4 + l, r), site(6 + l, r)
            f2 = spread(area[BOND2, r, l : l + 1, at])
            outs.append(
                site(a, r) * v(a, 0, 0) + f0 * v(b, 0, 0) + f1 * v(b, -1, 0) + f2 * v(b, 0, -1)
            )
            outs.append(
                site(b, r) * v(b, 0, 0)
                + f0 * v(a, 0, 0)
                + site(6 + l, r + 1) * v(a, 1, 0)
                + spread(bond_t[r, l : l + 1, at]) * v(a, 0, 1)
            )
        for s in range(2):
            for c in range(CODES):
                t, e, f = c // 9, c % 9 // 3 - 1, c % 3 - 1
                n = 8 * (f + 1) + 3 * t + e + 1
                outs[s] = outs[s] + spread(weights[r, s, n : n + 1, at]) * v(2 + t, e, f)
                if f == 0:
                    other = weights[r - e, s, n : n + 1, at]
                else:
                    n = 4 * (f + 1) + 3 * t + e + 1
                    other = weights_t[r - e, s, n : n + 1, at]
                outs[2 + t] = outs[2 + t] + spread(other) * v(s, -e, -f)
        return outs

    def advance(k, r):
        inside = jnp.where((r >= RIM) & (r < RIM + rows), 1.0, 0.0).astype(jnp.float32)
        cross, square, first_sum = zero, zero, zero
        turns = [{} for _ in range(4)]

        def store_turn(o, way, b):
            near = turns[o][b][(way + 1) // 2]
            if 0 <= b + way < blocks:
                near = jnp.where(first if way < 0 else last, turns[o][b + way][(way + 1) // 2], near)
            moved[k + 1][(way + 1) // 2, o, r, :, block(b)] = near

        for b in range(blocks):
            at = block(b)
            outs = hamiltonian(k, r, at)
            crosses, squares = zero, zero
            for o in range(4):
                old = term(k, o, r, at)
                new = outs[o] if k == 0 else 2.0 * outs[o] - term(k - 1, o, r, at)
                terms[k][o, r, :, at] = new
                crosses = crosses + new * old
                squares = squares + new * new
                if k == 0:
                    first_sum = first_sum + old * old
                if k < 2:
                    turns[o][b] = (back(new), ahead(new))
                    store_turn(o, -1, b)
                    if b > 0:
                        store_turn(o, 1, b - 1)
            if b == 0:
                crosses, squares = (jnp.where(lane > k, x, 0.0) for x in (crosses, squares))
            if b == blocks - 1:
                crosses, squares = (jnp.where(lane < LANES - 1 - k, x, 0.0) for x in (crosses, squares))
            cross, square = cross + crosses, square + squares
        if k < 2:
            for o in range(4):
                store_turn(o, 1, blocks - 1)
        if k == 0:
            sums[0] += inside * first_sum
        sums[2 * k + 1] += inside * cross
        sums[2 * k + 2] += inside * square

    def strip_terms(n):
        sides = [
            [halo[3 * (1 - n) + m, i] for i in range(3)] for m in range(3)
        ]
        side = [
            jnp.where(
                above[0], shift(sides[0][i], -WIDE * rows), jnp.where(below[0], shift(sides[2][i], WIDE * rows), sides[1][i])
            )
            for i in range(3)
        ]
        turns = (0, -STEPS, -2 * STEPS) if n == 0 else (0, -STEPS, STEPS)
        fields = []
        for g in range(8):
            m, j = divmod(8 * n + g, 4)
            top = shift(tile_halo[0, m], -32 * j - STEPS * n)
            bottom = shift(tile_halo[1, m], WIDE * (STEPS + rows) - 32 * j - STEPS * n)
            x = jnp.where(above[n], top, jnp.where(below[n], bottom, strips[n, g]))
            fields.append(jnp.where(mids if n else lefts, shift(side[g // 3], turns[g % 3]), x))
        strip_site[n, 0], strip_site[n, 1] = fields[SITE], fields[BOND2]
        strips[n, HOP], strips[n, CODE] = fields[HOP], fields[CODE]
        for s in range(2):
            totals = weigh_of(lambda f: strips[n, CODE, f : f + 1], lambda f: strips[n, HOP, f : f + 1], s)
            for g in range(3):
                strip_weights[n, s, 8 * g : 8 * g + 8] = totals[g]

        def spread(x):
            return jnp.broadcast_to(x, (8, LANES))

        def at(x, e, f):
            return shift(x, -(WIDE * e + f))

        def apply(v):
            outs = [None] * 4
            for l in range(2):
                a, b = 2 * l, 2 * l + 1
                sa, sb, f0, f1 = (spread(strip_site[n, 0, i : i + 1]) for i in (a, b, 4 + l, 6 + l))
                f2 = spread(strip_site[n, 1, l : l + 1])
                outs[a] = sa * v[a] + f0 * v[b] + f1 * at(v[b], -1, 0) + f2 * at(v[b], 0, -1)
                outs[b] = sb * v[b] + f0 * v[a] + at(f1 * v[a], 1, 0) + at(f2 * v[a], 0, 1)
            for c in range(CODES):
                t, e, f = c // 9, c % 9 // 3 - 1, c % 3 - 1
                i = 8 * (f + 1) + 3 * t + e + 1
                w = [spread(strip_weights[n, s, i : i + 1]) for s in range(2)]
                far = at(v[2 + t], e, f)
                for s in range(2):
                    outs[s] = outs[s] + w[s] * far
                outs[2 + t] = outs[2 + t] + at(w[0] * v[0] + w[1] * v[1], -e, -f)
            return outs

        older, old = None, fields[0:4]
        for k in range(3):
            outs = apply(old)
            new = outs if k == 0 else [2.0 * outs[o] - older[o] for o in range(4)]
            col = strip_col[n] - (STEPS if n == 0 else 0)
            wanted = (col >= 0) & (col <= k) if n == 0 else (col >= 5 - k) & (col <= 5)
            wanted = wanted & ~above[n] & ~below[n]
            cross = functools.reduce(jnp.add, [new[o] * old[o] for o in range(4)])
            square = functools.reduce(jnp.add, [new[o] * new[o] for o in range(4)])
            sums[2 * k + 1] += jnp.where(wanted, cross, 0.0)
            sums[2 * k + 2] += jnp.where(wanted, square, 0.0)
            older, old = old, new
        for o in range(4):
            strips[n, o] = old[o]

    loop(0, 2, lambda i: advance(0, low + 1 + i * (rows - 3)))
    rim(2, far).start()
    rim(2, near).start()
    loop(low + 2, high - 2, functools.partial(advance, 0))
    relay_on()
    for k in (1, 2):
        loop(low + 1 + k, high - 1 - k, functools.partial(advance, k))

    def rims(i):
        way = jnp.where(i == 0, far, near)
        row, out = edge(way)
        for layer in range(3):
            rim(layer, way).wait_recv()
            r = row + out * (min(layer, 1) + 1)
            if layer < 2:
                prepare(r, layer == 0)
                if layer == 0:
                    area[SITE, r + out, 6:8, 0:cols] = area[BOND2, r, 2:4, 0:cols]
            else:
                for o in range(4):
                    xs = [term1[o, r, :, block(b)] for b in range(blocks)]
                    own_turns(xs, -1, moved_at(moved1, (0, o, r)))
                    own_turns(xs, 1, moved_at(moved1, (1, o, r)))
            for k in range(1 if layer == 2 else 0, 3):
                advance(k, row + out * (layer - k))

    loop(0, 2, rims)
    for copy in pack_copies.values():
        copy.wait_recv()
    for copy in tile_copies:
        copy.wait_recv()
    for n in range(2):
        strip_terms(n)

    row = jnp.zeros((8, LANES), jnp.float32)
    for n in range(7):
        total = jnp.sum(sums[n], axis=1, keepdims=True)
        row = jnp.where(lane == sub + 8 * n, jnp.broadcast_to(total, (8, LANES)), row)
    part[...] = jnp.sum(row, axis=0, keepdims=True)
    all_parts[me] = part[...]

    def other(step):
        at = jnp.where(step > me, step, step - 1)
        return (lax.div(at, n_tile), lax.rem(at, n_tile))

    def part_copy(step):
        return pltpu.make_async_remote_copy(
            src_ref=part,
            dst_ref=all_parts.at[me],
            send_sem=part_send,
            recv_sem=part_recv,
            device_id=other(step),
            device_id_type=MESH,
        )

    while done[0] < len(rounds):
        relay_on()
    loop(1, devices, lambda i: part_copy(i).start())
    for o in range(4):
        both = jnp.where(lefts, strips[1, o], strips[0, o])
        for i in range(rows):
            x = shift(both, -(WIDE * (i + STEPS) + STEPS))
            term3[o, low + i, :, 0:LANES] = jnp.where(lane < STEPS, x, term3[o, low + i, :, 0:LANES])
            edge_at = slice(cols - LANES, cols)
            term3[o, low + i, :, edge_at] = jnp.where(lane >= LANES - STEPS, x, term3[o, low + i, :, edge_at])
    for o in range(4):
        out_ref[:, o] = jnp.swapaxes(term3[o, own, :, 0:cols], 0, 1)

    for copy in (*pack_copies.values(), *tile_copies):
        copy.wait_send()
    for layer in range(3):
        for way in range(2):
            rim(layer, way).wait_send()
    arrived = pltpu.make_async_remote_copy(
        src_ref=all_parts.at[1:devices],
        dst_ref=all_parts.at[1:devices],
        send_sem=part_send,
        recv_sem=part_recv,
        device_id=device(1),
        device_id_type=MESH,
    )
    arrived.wait_recv()
    arrived.wait_send()
    pieces = [all_parts[n] for n in range(devices)]
    while len(pieces) > 1:
        half_way = (len(pieces) + 1) // 2
        pieces = [
            pieces[n] + pieces[n + half_way] if n + half_way < len(pieces) else pieces[n]
            for n in range(half_way)
        ]
    total = pieces[0]
    total = jnp.broadcast_to(total / orbitals, (8, LANES))
    scaled = [pltpu.roll(total, (LANES - 8 * n) % LANES, 1)[0:1, 0:8] for n in range(7)]
    mom_ref[0:1, :] = scaled[0]
    mom_ref[1:2, :] = scaled[1]
    for n in range(2, 7):
        mom_ref[n : n + 1, :] = 2.0 * scaled[n] - scaled[n % 2]


def emit(last_ref, rows_ref, out_ref, mom_ref, sem):
    copies = [
        pltpu.make_async_copy(last_ref, out_ref, sem.at[0]),
        pltpu.make_async_copy(rows_ref, mom_ref, sem.at[1]),
    ]
    for copy in copies:
        copy.start()
    for copy in copies:
        copy.wait()


def on_device(n_col, n_tile, vectors, onsite, intra_hop, inter_index, inter_hop):
    count, _, rows, cols = vectors.shape
    slots = inter_index.shape[0]
    assert n_col > 2 and n_tile > 2
    assert count == 8 and slots == 4 and rows == 8 and cols % LANES == 0
    tall = rows + 2 * RIM
    ring = cols + LANES
    f32 = jnp.float32
    vmem = pl.BlockSpec(memory_space=pltpu.VMEM)
    dma = pltpu.SemaphoreType.DMA
    results = pl.pallas_call(
        functools.partial(kernel, n_col, n_tile, 4 * rows * cols * n_col * n_tile),
        out_shape=(
            jax.ShapeDtypeStruct(vectors.shape, f32),
            jax.ShapeDtypeStruct((7, count), f32),
        ),
        in_specs=[pl.BlockSpec(memory_space=pltpu.HBM)] * 5,
        out_specs=(vmem, vmem),
        scratch_shapes=[
            pltpu.VMEM(vectors.shape, f32),
            pltpu.VMEM(onsite.shape, f32),
            pltpu.VMEM((6, rows, cols), f32),
            pltpu.VMEM((2 * slots, rows, cols), jnp.int32),
            pltpu.VMEM((2 * slots, rows, cols), f32),
            dma((5,)),
            pltpu.VMEM((8, tall, 8, ring), f32),
            *[pltpu.VMEM((4, tall, 8, ring), f32)] * 3,
            *[pltpu.VMEM((2, 4, tall, 8, ring), f32)] * 3,
            pltpu.VMEM((tall, 2, 24, ring), f32),
            pltpu.VMEM((tall, 2, 16, ring), f32),
            pltpu.VMEM((tall, 8, ring), f32),
            pltpu.VMEM((2, 3, 8, LANES), f32),
            pltpu.VMEM((6, 3, 8, LANES), f32),
            pltpu.VMEM((2, 4, 8, LANES), f32),
            pltpu.VMEM((2, 4, 8, LANES), f32),
            pltpu.VMEM((2, 8, 8, LANES), f32),
            pltpu.VMEM((2, 2, 8, LANES), f32),
            pltpu.VMEM((2, 2, 24, LANES), f32),
            pltpu.VMEM((7, 8, LANES), f32),
            pltpu.VMEM((1, LANES), f32),
            pltpu.VMEM((n_col * n_tile, 1, LANES), f32),
            dma((3, 2)), dma((3, 2)), dma((6,)), dma((6,)), dma((2,)), dma((2,)), dma, dma,
            pltpu.SemaphoreType.REGULAR((len(relay_rounds(n_col, n_tile)),)),
        ],
        compiler_params=pltpu.CompilerParams(
            collective_id=0, has_side_effects=True, vmem_limit_bytes=32 << 20
        ),
    )(
        *(
            pltpu.with_memory_space_constraint(x, pltpu.HBM)
            for x in (
                vectors,
                onsite,
                intra_hop.reshape(6, rows, cols),
                inter_index.reshape(2 * slots, rows, cols),
                inter_hop.reshape(2 * slots, rows, cols),
            )
        )
    )
    kept = pl.BlockSpec(memory_space=pl.ANY)
    return pl.pallas_call(
        emit,
        out_shape=(
            jax.ShapeDtypeStruct(vectors.shape, f32),
            jax.ShapeDtypeStruct((7, count), f32),
        ),
        in_specs=[kept] * 2,
        out_specs=(kept, kept),
        scratch_shapes=[dma((2,))],
        compiler_params=pltpu.CompilerParams(vmem_limit_bytes=1 << 20),
    )(*results)


def solution(mesh):
    spec4, spec3 = P(None, None, "tile", "col"), P(None, "tile", "col")
    return jax.shard_map(
        functools.partial(on_device, mesh.shape["col"], mesh.shape["tile"]),
        mesh=mesh,
        in_specs=(spec4, spec3, spec4, spec4, spec4),
        out_specs=(spec4, P()),
        check_vma=False,
    )
```
